256 devices in a mesh: row: 8 (over z_lo, x), col: 32 (over y, z_hi, core).
Axes of the slice: x: 4, y: 4, z: 8 (z_hi: 4, z_lo: 2; z = z_hi * 2 + z_lo), core: 2. Of those that a mesh axis runs over, the one named last changes fastest.
Arguments:
- features: float32 [8192, 256], P(('row', 'col')), may hold values from -4 to 4
- neighbors: int32 [8192, 10], P(('row', 'col')), may hold values from 0 to 8191
- pivot: int32 [1], replicated, may hold values from 0 to 31
Outputs:
- distances: float32 [8192, 8192], P('row', 'col')
The draws below stay inside these ranges and needn't reach their ends.
Inputs may be any that keep to these rules, and one draw needn't show every extreme that they name: `neighbors`: point indices; a list may repeat an index or name its own point. The pivot block holds the points pivot[0] * 256 onward.
All inputs are finite; a program needn't handle non-finite values.
Results may differ from the reference program's by a relative error of at most 0.00005.
Values sent between devices are 32-bit elements; how exact they have to be, the bound alone decides.
A program may use at most 64 MiB of HBM per device.

```python
import math
import jax
import jax.numpy as jnp
from jax import lax

F = 256
K = 10
PB = 256
SQUARINGS = 3
N = 8192


def draw_features(key, part):
    scale_key, entry_key = jax.random.split(jax.random.fold_in(key, 11))
    scales = jnp.exp(jax.random.uniform(scale_key, (N, 1), jnp.float32, math.log(0.25), math.log(4.0)))
    entries = jax.random.normal(entry_key, (N, F), jnp.float32)
    values = entries * scales * F ** (-0.5)
    return jnp.clip(values, -4.0, 4.0).astype(jnp.float32)


def set_ends(drawn, stream_key, smallest, top_value):
    shape = drawn.shape
    index_at = [jax.random.randint(jax.random.fold_in(stream_key, axis), (), 0, shape[axis]) for axis in range(len(shape))]
    drawn = drawn.at[tuple(index_at)].set(smallest)
    longest = shape.index(max(shape))
    index_at[longest] = (index_at[longest] + 1) % shape[longest]
    return drawn.at[tuple(index_at)].set(top_value)


def setup_inputs(seed: int = 0) -> dict:
    arg_keys = jax.random.split(jax.random.key(seed), 4)
    return {
        "features": draw_features(jax.random.fold_in(arg_keys[3], 71), 0),
        "neighbors": set_ends(jax.random.randint(arg_keys[1], (N, K), 0, N), jax.random.fold_in(arg_keys[1], 1), 0, N - 1).astype(jnp.int32),
        "pivot": jax.random.randint(arg_keys[2], (1,), 0, N // PB).astype(jnp.int32),
    }


far_weight = 3.0

def weights_of(points_a, lists_a, ids_a, points_b, lists_b, ids_b):
    norm_a = lax.optimization_barrier(jnp.sum(points_a * points_a, axis=1))
    norm_b = lax.optimization_barrier(jnp.sum(points_b * points_b, axis=1))
    inner = jnp.einsum('if,jf->ij', points_a, points_b, precision=lax.Precision.HIGHEST)
    squares = norm_a[:, None] + norm_b[None, :] - 2.0 * inner
    length = jnp.sqrt(jnp.maximum(squares, 0.0))
    linked = jnp.zeros(squares.shape, dtype=bool)
    for slot in range(lists_a.shape[1]):
        linked = linked | (lists_a[:, slot][:, None] == ids_b[None, :])
        linked = linked | (lists_b[:, slot][None, :] == ids_a[:, None])
    weighted = jnp.where(linked, length, far_weight * length)
    return jnp.where(ids_a[:, None] == ids_b[None, :], jnp.zeros_like(weighted), weighted)

def min_plus_rows(left, right):

    def step(index, best):
        column = lax.dynamic_slice_in_dim(left, index, 1, 1)
        row_piece = lax.dynamic_slice_in_dim(right, index, 1, 0)
        return jnp.minimum(best, column + row_piece)
    first = left[:, :1] + right[:1, :]
    return lax.fori_loop(1, left.shape[1], step, first)

def min_plus(left, right):
    total = left.shape[0]
    block = 256 if total % 256 == 0 else total
    pieces = left.reshape(total // block, block, left.shape[1])
    result = lax.map(lambda piece: min_plus_rows(piece, right), pieces)
    return result.reshape(total, right.shape[1])

def reference(features, neighbors, pivot):
    point_ids = jnp.arange(features.shape[0], dtype=jnp.int32)
    weights = weights_of(features, neighbors, point_ids, features, neighbors, point_ids)
    pivot_base = (pivot[0] * PB).astype(jnp.int32)
    closed = lax.dynamic_slice(weights, (pivot_base, pivot_base), (PB, PB))
    for turn in range(SQUARINGS):
        closed = jnp.minimum(closed, min_plus(closed, closed))
    row_raw = lax.dynamic_slice_in_dim(weights, pivot_base, PB, 0)
    col_raw = lax.dynamic_slice_in_dim(weights, pivot_base, PB, 1)
    row_panel = jnp.minimum(row_raw, min_plus(closed, row_raw))
    col_panel = jnp.minimum(col_raw, min_plus(col_raw, closed))
    return jnp.minimum(weights, min_plus(col_panel, row_panel))
```

```python
import functools

import jax
import jax.numpy as jnp
from jax import lax
from jax.experimental import pallas as pl
from jax.experimental.pallas import tpu as pltpu
from jax.sharding import PartitionSpec as P

PB = 256
SQUARINGS = 3
K = 10
far_weight = 3.0
LANES = 128


def copy_for_each(value, axis):
    size = lax.axis_size(axis)
    return lax.all_to_all(
        jnp.broadcast_to(value[None], (size, *value.shape)), axis, 0, 0, tiled=True
    )


def joined_along(pieces, dim):
    dims = list(pieces.shape[1:])
    dims[dim] *= pieces.shape[0]
    return jnp.moveaxis(pieces, 0, dim).reshape(dims)


def collect(value, axis, dim):
    pieces = copy_for_each(value, axis)
    return joined_along(pieces, dim)


def picked(value, axis, root):
    return lax.dynamic_index_in_dim(lax.all_gather(value, axis), root, 0, keepdims=False)


def dot_nt(a, b):
    return lax.dot_general(
        a, b, (((1,), (1,)), ((), ())),
        precision=lax.Precision.HIGHEST, preferred_element_type=jnp.float32,
    )


def lane_norms(points):
    ones = jnp.ones((8, points.shape[1]), jnp.float32)
    return dot_nt(ones, points * points)[:1]


def weigh(pts_a, lists_a, base_a, pts_b, lists_bt, norm_b, base_b, out, step=32):
    width = pts_b.shape[0]

    def chunk(t, carry):
        rows = pl.ds(pl.multiple_of(t * step, step), step)
        a = pts_a[rows, :]
        norm_a = jnp.sum(a * a, axis=1, keepdims=True)
        inner = dot_nt(a, pts_b[...])
        squares = norm_a + norm_b[...] - 2.0 * inner
        length = jnp.sqrt(jnp.maximum(squares, 0.0))
        ids_a = base_a + t * step + lax.broadcasted_iota(jnp.int32, (step, width), 0)
        ids_b = base_b + lax.broadcasted_iota(jnp.int32, (step, width), 1)
        la = lists_a[rows, :]
        linked = ids_a == ids_b
        for slot in range(K):
            linked = linked | (la[:, slot : slot + 1] == ids_b)
            linked = linked | (lists_bt[slot : slot + 1, :] == ids_a)
        weighted = jnp.where(linked, length, far_weight * length)
        weighted = jnp.where(ids_a == ids_b, 0.0, weighted)
        for tile in range(width // LANES):
            out[tile, rows, :] = weighted[:, tile * LANES : (tile + 1) * LANES]
        return carry

    lax.fori_loop(0, pts_a.shape[0] // step, chunk, 0)


def min_plus(left, right, init, out, rows, first, count, tiles):
    halves = left.shape[0]
    split = (rows // 8, 8, LANES)

    def block(t, carry):
        at = pl.ds(pl.multiple_of((first + t) * rows, rows), rows)

        def half(h, best):
            piece = left[h, at, :].reshape(split)
            best = list(best)
            base = h * LANES
            for k in range(LANES):
                down = jnp.broadcast_to(piece[:, :, k : k + 1], split)
                for n, tile in enumerate(tiles):
                    row = right[tile, pl.ds(base + k, 8, stride=0), :]
                    best[n] = jnp.minimum(best[n], down + row[None])
            return tuple(best)

        best = tuple(init[tile, at, :].reshape(split) for tile in tiles)
        best = lax.fori_loop(0, halves, half, best)
        for n, tile in enumerate(tiles):
            out[tile, at, :] = best[n].reshape(rows, LANES)
        return carry

    lax.fori_loop(0, count, block, 0)


def body(base, rp, rlt, cp, cl, clt, pp, plists, plt_, o_ref, ct, bt, ka, kb, xt, wt, nr, npv, nc):
    row_base, col_base, pivot_base = base[0], base[1], base[2]
    npv[...] = lane_norms(pp[...])
    nr[...] = lane_norms(rp[...])
    weigh(pp, plists, pivot_base, pp, plt_, npv, pivot_base, ka)
    for turn in range(SQUARINGS + 1):
        src, dst = (ka, kb) if turn % 2 == 0 else (kb, ka)
        min_plus(src, src, src, dst, 128, 0, 1, (0, 1))
        min_plus(src, src, src, dst, 128, 1, 1, (1,))
        dst[0, 128:256, :] = dst[1, 0:128, :].T
    closed = ka if (SQUARINGS + 1) % 2 == 0 else kb
    weigh(cp, cl, col_base, pp, plt_, npv, pivot_base, bt)
    min_plus(bt, closed, bt, xt, 128, 0, 2, (0, 1))
    weigh(pp, plists, pivot_base, rp, rlt, nr, row_base, ct)
    weigh(cp, cl, col_base, rp, rlt, nr, row_base, wt)
    min_plus(xt, ct, wt, wt, 32, 0, 8, tuple(range(8)))
    for t in range(8):
        o_ref[t * LANES : (t + 1) * LANES, :] = wt[t].T


def tile_of(base, rp, rl, cp, cl, pp, plists):
    rows, cols = rp.shape[0], cp.shape[0]

    def across(lists):
        return jnp.pad(lists.T, ((0, 16 - K), (0, 0)))

    def down(lists):
        return jnp.pad(lists, ((0, 0), (0, LANES - K)))

    vmem = pl.BlockSpec(memory_space=pltpu.VMEM)
    f32 = jnp.float32
    return pl.pallas_call(
        body,
        out_shape=jax.ShapeDtypeStruct((rows, cols), f32),
        in_specs=[pl.BlockSpec(memory_space=pltpu.SMEM)] + [vmem] * 8,
        out_specs=vmem,
        scratch_shapes=[
            pltpu.VMEM((rows // LANES, PB, LANES), f32),
            pltpu.VMEM((PB // LANES, cols, LANES), f32),
            pltpu.VMEM((PB // LANES, PB, LANES), f32),
            pltpu.VMEM((PB // LANES, PB, LANES), f32),
            pltpu.VMEM((PB // LANES, cols, LANES), f32),
            pltpu.VMEM((rows // LANES, cols, LANES), f32),
            pltpu.VMEM((1, rows), f32),
            pltpu.VMEM((1, PB), f32),
            pltpu.VMEM((1, cols), f32),
        ],
        compiler_params=pltpu.CompilerParams(vmem_limit_bytes=40 << 20),
    )(base, rp, across(rl), cp, down(cl), across(cl), pp, down(plists), across(plists))


def local(features, neighbors, pivot):
    row_points, row_lists = (collect(features, "col", 0), collect(neighbors, "col", 0))
    row_count = row_points.shape[0]
    col_count = row_count * lax.axis_size("row") // lax.axis_size("col")
    row_index = lax.axis_index("row")
    col_index = lax.axis_index("col")
    offset = jnp.clip(col_index * col_count - row_index * row_count, 0, row_count - col_count)
    col_points = lax.dynamic_slice_in_dim(row_points, offset, col_count, 0)
    col_lists = lax.dynamic_slice_in_dim(row_lists, offset, col_count, 0)
    owner_row = col_index * col_count // row_count
    col_points, col_lists = (
        picked(col_points, "row", owner_row),
        picked(col_lists, "row", owner_row),
    )
    pivot_base = pivot[0] * PB
    pivot_row = pivot_base // row_count
    row_offset = jnp.clip(pivot_base - row_index * row_count, 0, row_count - PB)
    pivot_feats = lax.dynamic_slice_in_dim(row_points, row_offset, PB, 0)
    pivot_lists = lax.dynamic_slice_in_dim(row_lists, row_offset, PB, 0)
    pivot_feats, pivot_lists = (
        picked(pivot_feats, "row", pivot_row),
        picked(pivot_lists, "row", pivot_row),
    )
    base = jnp.stack([row_index * row_count, col_index * col_count, pivot_base]).astype(jnp.int32)
    return tile_of(base, row_points, row_lists, col_points, col_lists, pivot_feats, pivot_lists)


def solution(mesh):
    return jax.shard_map(
        local,
        mesh=mesh,
        in_specs=(P(("row", "col"), None), P(("row", "col"), None), P()),
        out_specs=P("row", "col"),
        check_vma=False,
    )
```

```python
import functools

import jax
import jax.numpy as jnp
from jax import lax
from jax.experimental import pallas as pl
from jax.experimental.pallas import tpu as pltpu
from jax.sharding import PartitionSpec as P

PB = 256
SQUARINGS = 3
K = 10
far_weight = 3.0
LANES = 128


def copy_for_each(value, axis):
    size = lax.axis_size(axis)
    return lax.all_to_all(
        jnp.broadcast_to(value[None], (size, *value.shape)), axis, 0, 0, tiled=True
    )


def joined_along(pieces, dim):
    dims = list(pieces.shape[1:])
    dims[dim] *= pieces.shape[0]
    return jnp.moveaxis(pieces, 0, dim).reshape(dims)


def collect(value, axis, dim):
    pieces = copy_for_each(value, axis)
    return joined_along(pieces, dim)


def picked(value, axis, root):
    return lax.dynamic_index_in_dim(lax.all_gather(value, axis), root, 0, keepdims=False)


def dot(a, b, dims):
    return lax.dot_general(
        a, b, (dims, ((), ())),
        precision=lax.Precision.HIGHEST, preferred_element_type=jnp.float32,
    )


def norms_down(points, out):
    p = points[...]
    out[...] = dot(p * p, jnp.ones((p.shape[1], LANES), jnp.float32), ((1,), (0,)))


def norms_across(points, out):
    def chunk(t, carry):
        p = points[pl.ds(pl.multiple_of(t * LANES, LANES), LANES), :]
        out[t] = dot(jnp.ones((8, p.shape[1]), jnp.float32), p * p, ((1,), (1,)))
        return carry

    lax.fori_loop(0, points.shape[0] // LANES, chunk, 0)


def bits_of(lists, base, words):
    n = lists.shape[1]
    word = lax.broadcasted_iota(jnp.int32, (words, n), 0)
    found = jnp.zeros((words, n), jnp.int32)
    for slot in range(K):
        at = lists[slot : slot + 1, :] - base
        bit = jnp.left_shift(jnp.int32(1), at & 31)
        found = found | jnp.where(jnp.right_shift(at, 5) == word, bit, 0)
    return found


def weigh(pts_a, lists_a, base_a, norm_a, pts_b, lists_b, base_b, norm_b, out, wa, wb):
    count, width = pts_a.shape[0], pts_b.shape[0]
    tiles = width // LANES

    bits = bits_of(lists_a, base_b, width // 32)
    pad = jnp.zeros((LANES - width // 32, count), jnp.int32)
    wa[...] = jnp.concatenate([bits, pad], axis=0).T
    bits = bits_of(lists_b, base_a, count // 32)
    for tile in range(tiles):
        wb[tile] = bits[:, tile * LANES : (tile + 1) * LANES]

    a = pts_a[...]

    def products(t, carry):
        b = pts_b[pl.ds(pl.multiple_of(t * 256, 256), 256), :]
        inner = dot(a, b, ((1,), (1,)))
        out[2 * t] = inner[:, :LANES]
        out[2 * t + 1] = inner[:, LANES:]
        return carry

    lax.fori_loop(0, width // 256, products, 0)

    lane = lax.broadcasted_iota(jnp.int32, (32, LANES), 1)
    down = lax.broadcasted_iota(jnp.int32, (32, LANES), 0)

    def group(n, carry):
        t, g = n // (count // 32), n % (count // 32)
        rows = pl.ds(pl.multiple_of(g * 32, 32), 32)
        squares = norm_a[rows, :] + jnp.tile(norm_b[t], (4, 1)) - 2.0 * out[t, rows, :]
        squares = jnp.maximum(squares, 0.0)
        length = squares * lax.rsqrt(jnp.maximum(squares, 1.2e-38))
        listed = lanes_of(wa[rows, :], lane // 32 + 4 * t)
        listed = jnp.right_shift(listed, lane & 31)
        lists = jnp.tile(wb[t, pl.ds(g, 8, stride=0), :], (4, 1))
        listed = listed | jnp.right_shift(lists, down)
        weighted = jnp.where((listed & 1) == 1, length, far_weight * length)
        same = (down - lane) == (base_b - base_a + t * LANES - g * 32)
        out[t, rows, :] = jnp.where(same, 0.0, weighted)
        return carry

    lax.fori_loop(0, tiles * (count // 32), group, 0)


AHEAD = 6


def lanes_of(piece, index):
    dims = lax.GatherDimensionNumbers(
        offset_dims=(), collapsed_slice_dims=(1,), start_index_map=(1,),
        operand_batching_dims=(0,), start_indices_batching_dims=(0,),
    )
    return lax.gather(
        piece, index[:, :, None], dims, (1, 1), mode=lax.GatherScatterMode.PROMISE_IN_BOUNDS
    )


def min_plus(left, right, fold, done, unroll=32, rows=16, together=1):
    tiles, depth = right.shape[0], right.shape[1]
    halves = left.shape[0]
    depth = depth // halves
    subs = rows // 8
    pattern = lax.broadcasted_iota(jnp.int32, (8, LANES), 1) // (LANES // fold)

    def block(t, carry):
        at = pl.ds(pl.multiple_of(t * rows, rows), rows)
        best = tuple(jnp.full((8, LANES), jnp.inf, jnp.float32) for _ in range(tiles * subs))

        for h in range(halves):
            pieces = [
                left[h, pl.ds(pl.multiple_of(t * rows + 8 * s, 8), 8), :] for s in range(subs)
            ]

            def spread_of(at, u):
                index = (at + u * fold) & (LANES - 1)
                return tuple(lanes_of(piece, index) for piece in pieces)

            def some(c, carry):
                ahead, best = list(carry[0]), list(carry[1])
                first = pattern + c * (unroll * fold)
                for u in range(unroll):
                    ahead.append(spread_of(first, u + AHEAD))
                    downs = ahead.pop(0)
                    for tile in range(tiles):
                        row = right[tile, pl.ds(h * depth + c * unroll + u, 8, stride=0), :]
                        for s, down in enumerate(downs):
                            n = tile * subs + s
                            best[n] = jnp.minimum(best[n], down + row)
                return tuple(ahead), tuple(best)

            ahead = tuple(spread_of(pattern, u) for u in range(AHEAD))
            _, best = lax.fori_loop(0, depth // unroll, some, (ahead, best))
        done(at, [jnp.concatenate(best[n * subs : n * subs + subs], axis=0) for n in range(tiles)])
        return carry

    def blocks(t, carry):
        for n in range(together):
            block(t * together + n, carry)
        return carry

    lax.fori_loop(0, left.shape[1] // rows // together, blocks, 0)


FOLD = 4


def folded(wide, right):
    lane = lax.broadcasted_iota(jnp.int32, (PB // FOLD, LANES), 1) // (LANES // FOLD)
    for tile in range(wide.shape[0]):
        piece = wide[tile, pl.ds(0, PB // FOLD, stride=FOLD), :]
        for c in range(1, FOLD):
            other = wide[tile, pl.ds(c, PB // FOLD, stride=FOLD), :]
            piece = jnp.where(lane == c, other, piece)
        right[tile] = piece


def gathered(parts):
    group = lax.broadcasted_iota(jnp.int32, parts[0].shape, 1) // (LANES // FOLD)
    tile = parts[0]
    for c in range(1, FOLD):
        tile = jnp.where(group == c, parts[c], tile)
    return tile


def reduced(piece):
    piece = jnp.minimum(piece, pltpu.roll(piece, 64, 1))
    return jnp.minimum(piece, pltpu.roll(piece, 32, 1))


def spread(tiles, wide):
    lane = lax.broadcasted_iota(jnp.int32, (32, LANES), 1) % (LANES // FOLD)
    for g in range(wide.shape[0]):

        def chunk(t, carry):
            rows = pl.ds(pl.multiple_of(t * 32, 32), 32)
            piece = tiles[g // FOLD, rows, :]
            wide[g, rows, :] = lanes_of(piece, lane + 32 * (g % FOLD))
            return carry

        lax.fori_loop(0, PB // 32, chunk, 0)


def body(base, rp, rlt, cp, clt, pp, plt_, o_ref, ct, bt, ka, wide, fold, xt, wt,
         nra, npd, npa, ncd, wa, wb):
    row_base, col_base, pivot_base = base[0], base[1], base[2]
    norms_across(rp, nra)
    norms_across(pp, npa)
    norms_down(pp, npd)
    norms_down(cp, ncd)
    weigh(pp, plt_, pivot_base, npd, pp, plt_, pivot_base, npa, ka, wa, wb)
    spread(ka, wide)

    def square(turn, carry):
        folded(wide, fold)

        def done(at, best):
            best = [reduced(b) for b in best]
            for g in range(8):
                wide[g, at, :] = best[g]
            for tile in range(2):
                kept = gathered(best[FOLD * tile : FOLD * tile + FOLD])
                ka[tile, at, :] = jnp.minimum(ka[tile, at, :], kept)

        min_plus(ka, fold, FOLD, done)
        return carry

    lax.fori_loop(0, SQUARINGS + 1, square, 0)
    folded(wide, fold)
    weigh(cp, clt, col_base, ncd, pp, plt_, pivot_base, npa, bt, wa, wb)

    def done(at, best):
        best = [reduced(b) for b in best]
        for tile in range(2):
            kept = gathered(best[FOLD * tile : FOLD * tile + FOLD])
            xt[tile, at, :] = jnp.minimum(bt[tile, at, :], kept)

    min_plus(bt, fold, FOLD, done)
    weigh(pp, plt_, pivot_base, npd, rp, rlt, row_base, nra, ct, wa, wb)
    weigh(cp, clt, col_base, ncd, rp, rlt, row_base, nra, wt, wa, wb)

    def done(at, best):
        for tile in range(8):
            wt[tile, at, :] = jnp.minimum(wt[tile, at, :], best[tile])

    min_plus(xt, ct, 1, done)
    for t in range(8):
        o_ref[t * LANES : (t + 1) * LANES, :] = wt[t].T


def tile_of(base, rp, rl, cp, cl, pp, plists):
    rows, cols = rp.shape[0], cp.shape[0]

    def across(lists):
        return jnp.pad(lists.T, ((0, 16 - K), (0, 0)))

    vmem = pl.BlockSpec(memory_space=pltpu.VMEM)
    f32 = jnp.float32
    return pl.pallas_call(
        body,
        out_shape=jax.ShapeDtypeStruct((rows, cols), f32),
        in_specs=[pl.BlockSpec(memory_space=pltpu.SMEM)] + [vmem] * 6,
        out_specs=vmem,
        scratch_shapes=[
            pltpu.VMEM((rows // LANES, PB, LANES), f32),
            pltpu.VMEM((PB // LANES, cols, LANES), f32),
            pltpu.VMEM((PB // LANES, PB, LANES), f32),
            pltpu.VMEM((2 * FOLD, PB, LANES), f32),
            pltpu.VMEM((2 * FOLD, PB // FOLD, LANES), f32),
            pltpu.VMEM((PB // LANES, cols, LANES), f32),
            pltpu.VMEM((rows // LANES, cols, LANES), f32),
            pltpu.VMEM((rows // LANES, 8, LANES), f32),
            pltpu.VMEM((PB, LANES), f32),
            pltpu.VMEM((PB // LANES, 8, LANES), f32),
            pltpu.VMEM((cols, LANES), f32),
            pltpu.VMEM((PB, LANES), jnp.int32),
            pltpu.VMEM((rows // LANES, 8, LANES), jnp.int32),
        ],
        compiler_params=pltpu.CompilerParams(vmem_limit_bytes=40 << 20),
    )(base, rp, across(rl), cp, across(cl), pp, across(plists))


def local(features, neighbors, pivot):
    row_points, row_lists = (collect(features, "col", 0), collect(neighbors, "col", 0))
    row_count = row_points.shape[0]
    col_count = row_count * lax.axis_size("row") // lax.axis_size("col")
    row_index = lax.axis_index("row")
    col_index = lax.axis_index("col")
    offset = jnp.clip(col_index * col_count - row_index * row_count, 0, row_count - col_count)
    col_points = lax.dynamic_slice_in_dim(row_points, offset, col_count, 0)
    col_lists = lax.dynamic_slice_in_dim(row_lists, offset, col_count, 0)
    owner_row = col_index * col_count // row_count
    col_points, col_lists = (
        picked(col_points, "row", owner_row),
        picked(col_lists, "row", owner_row),
    )
    pivot_base = pivot[0] * PB
    pivot_row = pivot_base // row_count
    row_offset = jnp.clip(pivot_base - row_index * row_count, 0, row_count - PB)
    pivot_feats = lax.dynamic_slice_in_dim(row_points, row_offset, PB, 0)
    pivot_lists = lax.dynamic_slice_in_dim(row_lists, row_offset, PB, 0)
    pivot_feats, pivot_lists = (
        picked(pivot_feats, "row", pivot_row),
        picked(pivot_lists, "row", pivot_row),
    )
    base = jnp.stack([row_index * row_count, col_index * col_count, pivot_base]).astype(jnp.int32)
    return tile_of(base, row_points, row_lists, col_points, col_lists, pivot_feats, pivot_lists)


def solution(mesh):
    return jax.shard_map(
        local,
        mesh=mesh,
        in_specs=(P(("row", "col"), None), P(("row", "col"), None), P()),
        out_specs=P("row", "col"),
        check_vma=False,
    )
```

```python
import functools

import jax
import jax.numpy as jnp
from jax import lax
from jax.experimental import pallas as pl
from jax.experimental.pallas import tpu as pltpu
from jax.sharding import PartitionSpec as P

MESH = pl.DeviceIdType.MESH
PB = 256
SQUARINGS = 3
K = 10
far_weight = 3.0
LANES = 128
SHARE = 32
PIECE = SHARE + 8
FOLD = 4
F32 = jnp.float32


def place():
    row, col = lax.axis_index("row"), lax.axis_index("col")
    return row, col, col // 8, lax.rem(col, 8) // 2, lax.rem(col, 2)


def send(src, dst, out_sem, in_sem, to):
    copy = pltpu.make_async_remote_copy(
        src_ref=src, dst_ref=dst, send_sem=out_sem, recv_sem=in_sem,
        device_id=to, device_id_type=MESH,
    )
    copy.start()
    return copy


def arrival(slot, out_sem, in_sem, to):
    pltpu.make_async_remote_copy(
        src_ref=slot, dst_ref=slot, send_sem=out_sem, recv_sem=in_sem,
        device_id=to, device_id_type=MESH,
    ).wait_recv()


def greet(row, col, y, m, home, whole):
    barrier = pltpu.get_barrier_semaphore()

    def signal(to):
        pl.semaphore_signal(barrier, inc=1, device_id=to, device_id_type=MESH)

    for d in range(1, 8):
        signal((lax.rem(row + d, 8), col))
        signal((row, y * 8 + lax.rem(m + d, 8)))
        signal((lax.rem(row + d, 8), home))
        signal((col // 4, lax.rem(col, 4) * 8 + lax.rem(m + d, 8)))
    for d in range(1, 4):
        signal((row, lax.rem(y + d, 4) * 8 + m))

    @pl.when(jnp.logical_not(whole))
    def _():
        signal((row, home))
        signal((col // 4, lax.rem(col, 4) * 8 + m))
        pl.semaphore_wait(barrier, 33)

    @pl.when(whole)
    def _():
        pl.semaphore_wait(barrier, 31)


def exchange(pivot, own, rows, cols, pivots, first, second,
             own_sem, s1, r1, s2, r2, s3, r3, sc, rc, sz, rz, sy, ry, sp, rp):
    row, col, y, zh, core = place()
    m = zh * 2 + core
    at = core * 4 + zh
    home = row * 4 + y
    whole = home == col
    mine = rows.at[y * 2 + core, zh]

    locals_ = [
        pltpu.make_async_copy(own, mine, own_sem.at[0]),
        pltpu.make_async_copy(own, first.at[row], own_sem.at[1]),
    ]
    for copy in locals_:
        copy.start()
    greet(row, col, y, m, home, whole)

    sent = []
    for d in range(1, 8):
        to = (lax.rem(row + d, 8), col)
        sent.append(send(own, first.at[row], s1.at[d], r1.at[row], to))
    for d in range(1, 4):
        to = (row, y * 8 + lax.rem(zh + d, 4) * 2 + core)
        sent.append(send(own, mine, sz.at[d], rz.at[zh], to))

    for d in range(1, 8):
        k = lax.rem(row + d, 8)
        arrival(first.at[k], s1.at[d], r1.at[k], (k, col))
    for copy in locals_:
        copy.wait()
    chosen = pivot[0] // 4
    second[y] = first[chosen]
    for d in range(1, 4):
        to = (row, lax.rem(y + d, 4) * 8 + m)
        sent.append(send(second.at[y], second.at[y], s2.at[d], r2.at[y], to))

    for d in range(8):
        to = (lax.rem(row + d, 8), home)
        if d:
            sent.append(send(own, cols.at[at], sc.at[d], rc.at[at], to))
    out = pltpu.make_async_remote_copy(
        src_ref=own, dst_ref=cols.at[at], send_sem=sc.at[0], recv_sem=rc.at[at],
        device_id=(row, home), device_id_type=MESH,
    )
    keep = pltpu.make_async_copy(own, cols.at[at], own_sem.at[2])

    @pl.when(whole)
    def _():
        keep.start()

    @pl.when(jnp.logical_not(whole))
    def _():
        out.start()

    for d in range(1, 4):
        k = lax.rem(y + d, 4)
        arrival(second.at[k], s2.at[d], r2.at[k], (row, k * 8 + m))
    pivots[at] = second[lax.rem(pivot[0], 4)]
    for d in range(1, 8):
        to = (row, y * 8 + lax.rem(m + d, 8))
        sent.append(send(pivots.at[at], pivots.at[at], s3.at[d], r3.at[at], to))

    for d in range(1, 4):
        k = lax.rem(zh + d, 4)
        arrival(rows.at[y * 2 + core, k], sz.at[d], rz.at[k], (row, y * 8 + k * 2 + core))
    share = rows.at[y * 2 + core]
    partner = (row, y * 8 + zh * 2 + 1 - core)
    for d in range(1, 4):
        to = (row, lax.rem(y + d, 4) * 8 + m)
        sent.append(send(share, share, sy.at[d], ry.at[y], to))
    sent.append(send(share, share, sp.at[0], rp.at[y], partner))

    for d in range(1, 8):
        k = lax.rem(m + d, 8)
        slot = lax.rem(k, 2) * 4 + k // 2
        arrival(pivots.at[slot], s3.at[d], r3.at[slot], (row, y * 8 + k))
    for d in range(1, 4):
        k = lax.rem(y + d, 4)
        share = rows.at[k * 2 + core]
        arrival(share, sy.at[d], ry.at[k], (row, k * 8 + m))
        sent.append(send(share, share, sp.at[d], rp.at[k], partner))
    for d in range(1, 8):
        k = lax.rem(m + d, 8)
        slot = lax.rem(k, 2) * 4 + k // 2
        arrival(cols.at[slot], sc.at[d], rc.at[slot], (col // 4, lax.rem(col, 4) * 8 + k))

    @pl.when(whole)
    def _():
        keep.wait()

    @pl.when(jnp.logical_not(whole))
    def _():
        out.wait_send()
        arrival(cols.at[at], sc.at[0], rc.at[at], (col // 4, lax.rem(col, 4) * 8 + m))

    for k in range(4):
        share = rows.at[k * 2 + 1 - core]
        arrival(share, sp.at[k], rp.at[k], partner)
    for copy in sent:
        copy.wait_send()


def moved(piece, pivot):
    sem = pltpu.SemaphoreType.DMA
    vmem = pl.BlockSpec(memory_space=pltpu.VMEM)
    return pl.pallas_call(
        exchange,
        out_shape=[
            jax.ShapeDtypeStruct((8, 4, PIECE, PB), F32),
            jax.ShapeDtypeStruct((8, PIECE, PB), F32),
            jax.ShapeDtypeStruct((8, PIECE, PB), F32),
        ],
        in_specs=[pl.BlockSpec(memory_space=pltpu.SMEM), vmem],
        out_specs=[vmem] * 3,
        scratch_shapes=[
            pltpu.VMEM((8, PIECE, PB), F32),
            pltpu.VMEM((4, PIECE, PB), F32),
            sem((3,)),
            sem((8,)), sem((8,)), sem((4,)), sem((4,)), sem((8,)), sem((8,)),
            sem((8,)), sem((8,)), sem((4,)), sem((4,)), sem((4,)), sem((4,)),
            sem((4,)), sem((4,)),
        ],
        compiler_params=pltpu.CompilerParams(
            collective_id=0, has_side_effects=True, vmem_limit_bytes=16 << 20
        ),
    )(pivot, piece)


def dot(a, b, dims):
    return lax.dot_general(
        a, b, (dims, ((), ())),
        precision=lax.Precision.HIGHEST, preferred_element_type=F32,
    )


def points_of(pieces, tile):
    return pieces[tile, :, :SHARE, :].reshape(LANES, PB)


def lists_of(pieces, tile):
    both = pieces[tile, 0, SHARE:, :]
    for zh in range(1, 4):
        both = both + pieces[tile, zh, SHARE:, :]
    both = both.astype(jnp.int32)
    return jnp.concatenate([both[:, :LANES], both[:, LANES:]], axis=0)


def norms_down(points, out):
    for tile in range(2):
        p = points_of(points, tile)
        out[tile * LANES : (tile + 1) * LANES, :] = dot(
            p * p, jnp.ones((PB, LANES), F32), ((1,), (0,))
        )


def norms_across(points, out):
    def chunk(t, carry):
        p = points_of(points, t)
        out[t] = dot(jnp.ones((8, PB), F32), p * p, ((1,), (1,)))
        return carry

    lax.fori_loop(0, points.shape[0], chunk, 0)


def bits_of(lists, base, words):
    word = lax.broadcasted_iota(jnp.int32, (words, LANES), 0)
    found = jnp.zeros((words, LANES), jnp.int32)
    for slot in range(K):
        at = lists[slot : slot + 1, :] - base
        bit = jnp.left_shift(jnp.int32(1), at & 31)
        found = found | jnp.where(jnp.right_shift(at, 5) == word, bit, 0)
    return found


def lanes_of(piece, index):
    dims = lax.GatherDimensionNumbers(
        offset_dims=(), collapsed_slice_dims=(1,), start_index_map=(1,),
        operand_batching_dims=(0,), start_indices_batching_dims=(0,),
    )
    return lax.gather(
        piece, index[:, :, None], dims, (1, 1), mode=lax.GatherScatterMode.PROMISE_IN_BOUNDS
    )


def weigh(down_of, base_a, norm_a, across_of, base_b, norm_b, out, wa, wb):
    tiles = across_of.shape[0]
    for tile in range(2):
        bits = bits_of(lists_of(down_of, tile), base_b, 4 * tiles)
        pad = jnp.zeros((LANES - 4 * tiles, LANES), jnp.int32)
        wa[tile * LANES : (tile + 1) * LANES, :] = jnp.concatenate([bits, pad], axis=0).T

    def words(t, carry):
        wb[t] = bits_of(lists_of(across_of, t), base_a, 8)
        return carry

    lax.fori_loop(0, tiles, words, 0)
    a = jnp.concatenate([points_of(down_of, 0), points_of(down_of, 1)], axis=0)

    def products(t, carry):
        b = jnp.concatenate([points_of(across_of, 2 * t), points_of(across_of, 2 * t + 1)], axis=0)
        inner = dot(a, b, ((1,), (1,)))
        out[2 * t] = inner[:, :LANES]
        out[2 * t + 1] = inner[:, LANES:]
        return carry

    lax.fori_loop(0, tiles // 2, products, 0)

    lane = lax.broadcasted_iota(jnp.int32, (32, LANES), 1)
    inside = lane & 31
    across = (lane // 32) * 64 + inside
    down = lax.broadcasted_iota(jnp.int32, (32, LANES), 0)

    def group(n, carry):
        t, g = n // 8, n % 8
        rows = pl.ds(pl.multiple_of(g * 32, 32), 32)
        word_a = (t // 2) * 8 + t % 2
        word_b = (g % 4) * 2 + g // 4
        squares = norm_a[rows, :] + jnp.tile(norm_b[t], (4, 1)) - 2.0 * out[t, rows, :]
        squares = jnp.maximum(squares, 0.0)
        length = squares * lax.rsqrt(jnp.maximum(squares, 1.2e-38))
        listed = lanes_of(wa[rows, :], (lane // 32) * 2 + word_a)
        listed = jnp.right_shift(listed, inside)
        lists = jnp.tile(wb[t, pl.ds(word_b, 8, stride=0), :], (4, 1))
        listed = listed | jnp.right_shift(lists, down)
        weighted = jnp.where((listed & 1) == 1, length, far_weight * length)
        same = (down - across) == (base_b - base_a + 32 * (word_a - word_b))
        out[t, rows, :] = jnp.where(same, 0.0, weighted)
        return carry

    lax.fori_loop(0, tiles * 8, group, 0)


def min_plus(left, right, fold, done, rows):
    tiles = right.shape[0]
    halves = left.shape[0]
    depth = right.shape[1] // halves
    subs = rows // 8
    pattern = lax.broadcasted_iota(jnp.int32, (8, LANES), 1) // (LANES // fold)

    def block(t, carry):
        def rows_of(s):
            return pl.ds(pl.multiple_of(t * rows + 8 * s, 8), 8)

        def half(h, best):
            best = list(best)
            pieces = [left[h, rows_of(s), :] for s in range(subs)]
            for q in range(depth):
                downs = [lanes_of(piece, pattern + q * fold) for piece in pieces]
                for tile in range(tiles):
                    row = right[tile, pl.ds(h * depth + q, 8, stride=0), :]
                    for s in range(subs):
                        n = tile * subs + s
                        best[n] = jnp.minimum(best[n], downs[s] + row)
            return tuple(best)

        best = tuple(jnp.full((8, LANES), jnp.inf, F32) for _ in range(tiles * subs))
        best = lax.fori_loop(0, halves, half, best)
        for s in range(subs):
            done(rows_of(s), [best[tile * subs + s] for tile in range(tiles)])
        return carry

    lax.fori_loop(0, left.shape[1] // rows, block, 0)


def folded(wide, right):
    lane = lax.broadcasted_iota(jnp.int32, (PB // FOLD, LANES), 1) // (LANES // FOLD)
    for tile in range(wide.shape[0]):
        piece = wide[tile, pl.ds(0, PB // FOLD, stride=FOLD), :]
        for c in range(1, FOLD):
            other = wide[tile, pl.ds(c, PB // FOLD, stride=FOLD), :]
            piece = jnp.where(lane == c, other, piece)
        right[tile] = piece


def gathered(parts):
    group = lax.broadcasted_iota(jnp.int32, parts[0].shape, 1) // (LANES // FOLD)
    tile = parts[0]
    for c in range(1, FOLD):
        tile = jnp.where(group == c, parts[c], tile)
    return tile


def reduced(piece):
    piece = jnp.minimum(piece, pltpu.roll(piece, 64, 1))
    return jnp.minimum(piece, pltpu.roll(piece, 32, 1))


def spread(tiles, wide):
    lane = lax.broadcasted_iota(jnp.int32, (32, LANES), 1) % (LANES // FOLD)
    for g in range(wide.shape[0]):

        def chunk(t, carry):
            rows = pl.ds(pl.multiple_of(t * 32, 32), 32)
            piece = tiles[g // FOLD, rows, :]
            wide[g, rows, :] = lanes_of(piece, lane + 32 * (g % FOLD))
            return carry

        lax.fori_loop(0, PB // 32, chunk, 0)


def body(base, rb, cb, pb, o_ref, ct, bt, ka, wide, fold, xt, wt, nra, npd, npa, ncd, wa, wb):
    row_base, col_base, pivot_base = base[0], base[1], base[2]
    norms_across(rb, nra)
    norms_across(pb, npa)
    norms_down(pb, npd)
    norms_down(cb, ncd)
    weigh(pb, pivot_base, npd, pb, pivot_base, npa, ka, wa, wb)
    spread(ka, wide)

    def square(turn, carry):
        folded(wide, fold)

        def done(at, best):
            best = [reduced(b) for b in best]
            for g in range(8):
                wide[g, at, :] = best[g]
            for tile in range(2):
                kept = gathered(best[FOLD * tile : FOLD * tile + FOLD])
                ka[tile, at, :] = jnp.minimum(ka[tile, at, :], kept)

        min_plus(ka, fold, FOLD, done, 32)
        return carry

    lax.fori_loop(0, SQUARINGS + 1, square, 0)
    folded(wide, fold)
    weigh(cb, col_base, ncd, pb, pivot_base, npa, bt, wa, wb)

    def done(at, best):
        best = [reduced(b) for b in best]
        for tile in range(2):
            kept = gathered(best[FOLD * tile : FOLD * tile + FOLD])
            xt[tile, at, :] = jnp.minimum(bt[tile, at, :], kept)

    min_plus(bt, fold, FOLD, done, 32)
    weigh(pb, pivot_base, npd, rb, row_base, nra, ct, wa, wb)
    weigh(cb, col_base, ncd, rb, row_base, nra, wt, wa, wb)

    def done(at, best):
        for tile in range(8):
            wt[tile, at, :] = jnp.minimum(wt[tile, at, :], best[tile])

    min_plus(xt, ct, 1, done, 32)
    for t in range(8):
        for n in range(2):
            parts = [
                wt[t, (m % 2) * LANES + (m // 2) * 32 : (m % 2) * LANES + (m // 2) * 32 + 32, :]
                for m in range(4 * n, 4 * n + 4)
            ]
            flat = jnp.concatenate(parts, axis=0).T
            for zh in range(4):
                top = (t // 2) * 256 + (2 * zh + t % 2) * 32
                o_ref[top : top + 32, n * LANES : (n + 1) * LANES] = flat[zh * 32 : zh * 32 + 32]


def tile_of(base, rows, cols, pivots):
    vmem = pl.BlockSpec(memory_space=pltpu.VMEM)
    tiles = rows.shape[0]
    return pl.pallas_call(
        body,
        out_shape=jax.ShapeDtypeStruct((tiles * LANES, PB), F32),
        in_specs=[pl.BlockSpec(memory_space=pltpu.SMEM)] + [vmem] * 3,
        out_specs=vmem,
        scratch_shapes=[
            pltpu.VMEM((tiles, PB, LANES), F32),
            pltpu.VMEM((2, PB, LANES), F32),
            pltpu.VMEM((2, PB, LANES), F32),
            pltpu.VMEM((2 * FOLD, PB, LANES), F32),
            pltpu.VMEM((2 * FOLD, PB // FOLD, LANES), F32),
            pltpu.VMEM((2, PB, LANES), F32),
            pltpu.VMEM((tiles, PB, LANES), F32),
            pltpu.VMEM((tiles, 8, LANES), F32),
            pltpu.VMEM((PB, LANES), F32),
            pltpu.VMEM((2, 8, LANES), F32),
            pltpu.VMEM((PB, LANES), F32),
            pltpu.VMEM((PB, LANES), jnp.int32),
            pltpu.VMEM((tiles, 8, LANES), jnp.int32),
        ],
        compiler_params=pltpu.CompilerParams(vmem_limit_bytes=40 << 20),
    )(base, rows, cols, pivots)


def local(features, neighbors, pivot):
    row, col, y, zh, core = place()
    lists = jnp.zeros((16, LANES), F32)
    lists = lax.dynamic_update_slice(lists, neighbors.T.astype(F32), (0, zh * SHARE))
    lists = jnp.concatenate([lists[:8], lists[8:]], axis=1)
    piece = jnp.concatenate([features, lists], axis=0)
    rows, cols, pivots = moved(piece, pivot)
    base = jnp.stack([row * 1024, col * PB, pivot[0] * PB]).astype(jnp.int32)
    return tile_of(
        base, rows, cols.reshape(2, 4, PIECE, PB), pivots.reshape(2, 4, PIECE, PB)
    )


def solution(mesh):
    return jax.shard_map(
        local,
        mesh=mesh,
        in_specs=(P(("row", "col"), None), P(("row", "col"), None), P()),
        out_specs=P("row", "col"),
        check_vma=False,
    )
```

```python
import functools

import jax
import jax.numpy as jnp
from jax import lax
from jax.experimental import pallas as pl
from jax.experimental.pallas import tpu as pltpu
from jax.sharding import PartitionSpec as P

MESH = pl.DeviceIdType.MESH
PB = 256
SQUARINGS = 3
K = 10
far_weight = 3.0
LANES = 128
SHARE = 32
PIECE = SHARE + 8
FOLD = 4
F32 = jnp.float32


def place():
    row, col = lax.axis_index("row"), lax.axis_index("col")
    return row, col, col // 8, lax.rem(col, 8) // 2, lax.rem(col, 2)


def send(src, dst, out_sem, in_sem, to):
    copy = pltpu.make_async_remote_copy(
        src_ref=src, dst_ref=dst, send_sem=out_sem, recv_sem=in_sem,
        device_id=to, device_id_type=MESH,
    )
    copy.start()
    return copy


def arrival(slot, out_sem, in_sem, to):
    pltpu.make_async_remote_copy(
        src_ref=slot, dst_ref=slot, send_sem=out_sem, recv_sem=in_sem,
        device_id=to, device_id_type=MESH,
    ).wait_recv()


def greet(row, col, y, m):
    barrier = pltpu.get_barrier_semaphore()

    def signal(to):
        pl.semaphore_signal(barrier, inc=1, device_id=to, device_id_type=MESH)

    for d in range(1, 8):
        signal((lax.rem(row + d, 8), col))
        signal((row, y * 8 + lax.rem(m + d, 8)))
    for d in range(1, 4):
        signal((row, lax.rem(y + d, 4) * 8 + m))
    pl.semaphore_wait(barrier, 17)


def gather_and_close(pivot, own, rows, cols, pivots, closed, first, second, ka, wide, fold,
                     npd, npa, wa, wb, own_sem, s1, r1, s2, r2, s3, r3, s4, r4,
                     sc, rc, sz, rz, sy, ry, sp, rp, sf, rf):
    row, col, y, zh, core = place()
    m = zh * 2 + core
    home = row * 4 + y
    whole = home == col
    mine = rows.at[y * 2 + core, zh]
    partner = (row, y * 8 + zh * 2 + 1 - core)

    kept = [
        pltpu.make_async_copy(own, mine, own_sem.at[0]),
        pltpu.make_async_copy(own, first.at[row], own_sem.at[1]),
    ]
    for copy in kept:
        copy.start()
    greet(row, col, y, m)

    sent = []
    for d in range(1, 8):
        to = (lax.rem(row + d, 8), col)
        sent.append(send(own, first.at[row], s1.at[d], r1.at[row], to))
    for d in range(1, 4):
        to = (row, y * 8 + lax.rem(zh + d, 4) * 2 + core)
        sent.append(send(own, mine, sz.at[d], rz.at[zh], to))
    for d in range(1, 8):
        k = lax.rem(row + d, 8)
        arrival(first.at[k], s1.at[d], r1.at[k], (k, col))
    for copy in kept:
        copy.wait()
    second[y] = first[pivot[0] // 4]
    for d in range(1, 4):
        to = (row, lax.rem(y + d, 4) * 8 + m)
        sent.append(send(second.at[y], second.at[y], s2.at[d], r2.at[y], to))
    for d in range(1, 4):
        k = lax.rem(y + d, 4)
        arrival(second.at[k], s2.at[d], r2.at[k], (row, k * 8 + m))
    pivots[core, zh] = second[lax.rem(pivot[0], 4)]
    piece = pivots.at[core, zh]
    for d in range(1, 4):
        to = (row, y * 8 + lax.rem(zh + d, 4) * 2 + core)
        sent.append(send(piece, piece, s3.at[d], r3.at[zh], to))

    for d in range(1, 4):
        k = lax.rem(zh + d, 4)
        arrival(rows.at[y * 2 + core, k], sz.at[d], rz.at[k], (row, y * 8 + k * 2 + core))
    share = rows.at[y * 2 + core]
    for d in range(1, 4):
        to = (row, lax.rem(y + d, 4) * 8 + m)
        sent.append(send(share, share, sy.at[d], ry.at[y], to))

    for d in range(1, 4):
        k = lax.rem(zh + d, 4)
        arrival(pivots.at[core, k], s3.at[d], r3.at[k], (row, y * 8 + k * 2 + core))
    sent.append(send(pivots.at[core], pivots.at[core], s4.at[0], r4.at[0], partner))
    sent.append(send(share, share, sp.at[0], rp.at[y], partner))
    arrival(pivots.at[1 - core], s4.at[0], r4.at[0], partner)

    for d in range(1, 8):
        to = (lax.rem(row + d, 8), home)
        sent.append(send(own, cols.at[core, zh], sc.at[d], rc.at[m], to))
    out = pltpu.make_async_remote_copy(
        src_ref=own, dst_ref=cols.at[core, zh], send_sem=sc.at[0], recv_sem=rc.at[m],
        device_id=(row, home), device_id_type=MESH,
    )
    keep = pltpu.make_async_copy(own, cols.at[core, zh], own_sem.at[2])

    @pl.when(whole)
    def _():
        keep.start()

    @pl.when(jnp.logical_not(whole))
    def _():
        out.start()

    base = pivot[0] * PB
    norms_across(pivots, npa)
    norms_down(pivots, npd)
    weigh(pivots, base, npd, pivots, base, npa, ka, wa, wb)
    spread(ka, wide)
    folded(wide, fold.at[0], 0, PB // FOLD)
    top = core * LANES

    def square(turn, carry):
        old, new = lax.rem(turn, 2), lax.rem(turn + 1, 2)

        def done(at, best):
            best = [reduced(b) for b in best]
            for g in range(2 * FOLD):
                wide[g, at, :] = best[g]
            for tile in range(2):
                part = gathered(best[FOLD * tile : FOLD * tile + FOLD])
                ka[tile, at, :] = jnp.minimum(ka[tile, at, :], part)

        min_plus(ka, fold.at[old], FOLD, done, 32, top, LANES)
        half = LANES // FOLD
        low = pl.multiple_of(core * half, half)
        folded(wide.at[:, pl.ds(pl.multiple_of(top, LANES), LANES)], fold.at[new], low, half)
        ours = fold.at[new, :, pl.ds(low, half)]
        theirs = fold.at[new, :, pl.ds(pl.multiple_of(half - low, half), half)]
        copy = send(ours, ours, sf.at[new], rf.at[new], partner)
        arrival(theirs, sf.at[new], rf.at[new], partner)
        copy.wait_send()
        return carry

    lax.fori_loop(0, 1, square, 0)
    for d in range(1, 4):
        k = lax.rem(y + d, 4)
        share = rows.at[k * 2 + core]
        arrival(share, sy.at[d], ry.at[k], (row, k * 8 + m))
        sent.append(send(share, share, sp.at[d], rp.at[k], partner))
    lax.fori_loop(1, SQUARINGS + 1, square, 0)
    closed[...] = fold[(SQUARINGS + 1) % 2]

    for d in range(1, 8):
        k = lax.rem(m + d, 8)
        slot = cols.at[lax.rem(k, 2), k // 2]
        arrival(slot, sc.at[d], rc.at[k], (col // 4, lax.rem(col, 4) * 8 + k))

    @pl.when(whole)
    def _():
        keep.wait()

    @pl.when(jnp.logical_not(whole))
    def _():
        out.wait_send()

    for k in range(4):
        arrival(rows.at[k * 2 + 1 - core], sp.at[k], rp.at[k], partner)

    @pl.when(jnp.logical_not(whole))
    def _():
        arrival(cols.at[core, zh], sc.at[0], rc.at[m], (col // 4, lax.rem(col, 4) * 8 + m))

    for copy in sent:
        copy.wait_send()


def moved(piece, pivot):
    sem = pltpu.SemaphoreType.DMA
    vmem = pl.BlockSpec(memory_space=pltpu.VMEM)
    return pl.pallas_call(
        gather_and_close,
        out_shape=[
            jax.ShapeDtypeStruct((8, 4, PIECE, PB), F32),
            jax.ShapeDtypeStruct((2, 4, PIECE, PB), F32),
            jax.ShapeDtypeStruct((2, 4, PIECE, PB), F32),
            jax.ShapeDtypeStruct((2 * FOLD, PB // FOLD, LANES), F32),
        ],
        in_specs=[pl.BlockSpec(memory_space=pltpu.SMEM), vmem],
        out_specs=[vmem] * 4,
        scratch_shapes=[
            pltpu.VMEM((8, PIECE, PB), F32),
            pltpu.VMEM((4, PIECE, PB), F32),
            pltpu.VMEM((2, PB, LANES), F32),
            pltpu.VMEM((2 * FOLD, PB, LANES), F32),
            pltpu.VMEM((2, 2 * FOLD, PB // FOLD, LANES), F32),
            pltpu.VMEM((PB, LANES), F32),
            pltpu.VMEM((2, 8, LANES), F32),
            pltpu.VMEM((PB, LANES), jnp.int32),
            pltpu.VMEM((2, 8, LANES), jnp.int32),
            sem((3,)),
            sem((8,)), sem((8,)), sem((4,)), sem((4,)), sem((4,)), sem((4,)), sem((1,)), sem((1,)),
            sem((8,)), sem((8,)), sem((4,)), sem((4,)), sem((4,)), sem((4,)),
            sem((4,)), sem((4,)), sem((2,)), sem((2,)),
        ],
        compiler_params=pltpu.CompilerParams(
            collective_id=0, has_side_effects=True, vmem_limit_bytes=24 << 20
        ),
    )(pivot, piece)


def dot(a, b, dims):
    return lax.dot_general(
        a, b, (dims, ((), ())),
        precision=lax.Precision.HIGHEST, preferred_element_type=F32,
    )


def points_of(pieces, tile):
    return pieces[tile, :, :SHARE, :].reshape(LANES, PB)


def lists_of(pieces, tile):
    both = pieces[tile, 0, SHARE:, :]
    for zh in range(1, 4):
        both = both + pieces[tile, zh, SHARE:, :]
    both = both.astype(jnp.int32)
    return jnp.concatenate([both[:, :LANES], both[:, LANES:]], axis=0)


def norms_down(points, out):
    for tile in range(2):
        p = points_of(points, tile)
        out[tile * LANES : (tile + 1) * LANES, :] = dot(
            p * p, jnp.ones((PB, LANES), F32), ((1,), (0,))
        )


def norms_across(points, out):
    def chunk(t, carry):
        p = points_of(points, t)
        out[t] = dot(jnp.ones((8, PB), F32), p * p, ((1,), (1,)))
        return carry

    lax.fori_loop(0, points.shape[0], chunk, 0)


def bits_of(lists, base, words):
    word = lax.broadcasted_iota(jnp.int32, (words, LANES), 0)
    found = jnp.zeros((words, LANES), jnp.int32)
    for slot in range(K):
        at = lists[slot : slot + 1, :] - base
        bit = jnp.left_shift(jnp.int32(1), at & 31)
        found = found | jnp.where(jnp.right_shift(at, 5) == word, bit, 0)
    return found


def lanes_of(piece, index):
    dims = lax.GatherDimensionNumbers(
        offset_dims=(), collapsed_slice_dims=(1,), start_index_map=(1,),
        operand_batching_dims=(0,), start_indices_batching_dims=(0,),
    )
    return lax.gather(
        piece, index[:, :, None], dims, (1, 1), mode=lax.GatherScatterMode.PROMISE_IN_BOUNDS
    )


def weigh(down_of, base_a, norm_a, across_of, base_b, norm_b, out, wa, wb):
    tiles = across_of.shape[0]
    for tile in range(2):
        bits = bits_of(lists_of(down_of, tile), base_b, 4 * tiles)
        pad = jnp.zeros((LANES - 4 * tiles, LANES), jnp.int32)
        wa[tile * LANES : (tile + 1) * LANES, :] = jnp.concatenate([bits, pad], axis=0).T

    def words(t, carry):
        wb[t] = bits_of(lists_of(across_of, t), base_a, 8)
        return carry

    lax.fori_loop(0, tiles, words, 0)
    a = jnp.concatenate([points_of(down_of, 0), points_of(down_of, 1)], axis=0)

    def products(t, carry):
        b = jnp.concatenate([points_of(across_of, 2 * t), points_of(across_of, 2 * t + 1)], axis=0)
        inner = dot(a, b, ((1,), (1,)))
        out[2 * t] = inner[:, :LANES]
        out[2 * t + 1] = inner[:, LANES:]
        return carry

    lax.fori_loop(0, tiles // 2, products, 0)

    lane = lax.broadcasted_iota(jnp.int32, (32, LANES), 1)
    inside = lane & 31
    across = (lane // 32) * 64 + inside
    down = lax.broadcasted_iota(jnp.int32, (32, LANES), 0)

    def group(n, carry):
        t, g = n // 8, n % 8
        rows = pl.ds(pl.multiple_of(g * 32, 32), 32)
        word_a = (t // 2) * 8 + t % 2
        word_b = (g % 4) * 2 + g // 4
        squares = norm_a[rows, :] + jnp.tile(norm_b[t], (4, 1)) - 2.0 * out[t, rows, :]
        squares = jnp.maximum(squares, 0.0)
        length = squares * lax.rsqrt(jnp.maximum(squares, 1.2e-38))
        listed = lanes_of(wa[rows, :], (lane // 32) * 2 + word_a)
        listed = jnp.right_shift(listed, inside)
        lists = jnp.tile(wb[t, pl.ds(word_b, 8, stride=0), :], (4, 1))
        listed = listed | jnp.right_shift(lists, down)
        weighted = jnp.where((listed & 1) == 1, length, far_weight * length)
        same = (down - across) == (base_b - base_a + 32 * (word_a - word_b))
        out[t, rows, :] = jnp.where(same, 0.0, weighted)
        return carry

    lax.fori_loop(0, tiles * 8, group, 0)


def min_plus(left, right, fold, done, rows, top, count):
    tiles = right.shape[0]
    halves = left.shape[0]
    depth = right.shape[1] // halves
    subs = rows // 8
    pattern = lax.broadcasted_iota(jnp.int32, (8, LANES), 1) // (LANES // fold)

    def block(t, carry):
        def rows_of(s):
            return pl.ds(pl.multiple_of(top + t * rows + 8 * s, 8), 8)

        def half(h, best):
            best = list(best)
            pieces = [left[h, rows_of(s), :] for s in range(subs)]
            for q in range(depth):
                downs = [lanes_of(piece, pattern + q * fold) for piece in pieces]
                for tile in range(tiles):
                    row = right[tile, pl.ds(h * depth + q, 8, stride=0), :]
                    for s in range(subs):
                        n = tile * subs + s
                        best[n] = jnp.minimum(best[n], downs[s] + row)
            return tuple(best)

        best = tuple(jnp.full((8, LANES), jnp.inf, F32) for _ in range(tiles * subs))
        best = lax.fori_loop(0, halves, half, best)
        for s in range(subs):
            done(rows_of(s), [best[tile * subs + s] for tile in range(tiles)])
        return carry

    lax.fori_loop(0, count // rows, block, 0)


def folded(wide, right, low, count):
    lane = lax.broadcasted_iota(jnp.int32, (count, LANES), 1) // (LANES // FOLD)
    for tile in range(wide.shape[0]):
        piece = wide[tile, pl.ds(0, count, stride=FOLD), :]
        for c in range(1, FOLD):
            other = wide[tile, pl.ds(c, count, stride=FOLD), :]
            piece = jnp.where(lane == c, other, piece)
        right[tile, pl.ds(low, count), :] = piece


def gathered(parts):
    group = lax.broadcasted_iota(jnp.int32, parts[0].shape, 1) // (LANES // FOLD)
    tile = parts[0]
    for c in range(1, FOLD):
        tile = jnp.where(group == c, parts[c], tile)
    return tile


def reduced(piece):
    piece = jnp.minimum(piece, pltpu.roll(piece, 64, 1))
    return jnp.minimum(piece, pltpu.roll(piece, 32, 1))


def spread(tiles, wide):
    lane = lax.broadcasted_iota(jnp.int32, (32, LANES), 1) & 31

    def chunk(t, carry):
        rows = pl.ds(pl.multiple_of(t * 32, 32), 32)
        for g in range(wide.shape[0]):
            wide[g, rows, :] = lanes_of(tiles[g // FOLD, rows, :], lane + 32 * (g % FOLD))
        return carry

    lax.fori_loop(0, PB // 32, chunk, 0)


def body(base, rb, cb, pb, fold, o_ref, ct, bt, xt, wt, nra, npd, npa, ncd, wa, wb):
    row_base, col_base, pivot_base = base[0], base[1], base[2]
    norms_across(rb, nra)
    norms_across(pb, npa)
    norms_down(pb, npd)
    norms_down(cb, ncd)
    weigh(cb, col_base, ncd, pb, pivot_base, npa, bt, wa, wb)

    def done(at, best):
        best = [reduced(b) for b in best]
        for tile in range(2):
            kept = gathered(best[FOLD * tile : FOLD * tile + FOLD])
            xt[tile, at, :] = jnp.minimum(bt[tile, at, :], kept)

    min_plus(bt, fold, FOLD, done, 32, 0, PB)
    weigh(pb, pivot_base, npd, rb, row_base, nra, ct, wa, wb)
    weigh(cb, col_base, ncd, rb, row_base, nra, wt, wa, wb)

    def done(at, best):
        for tile in range(8):
            wt[tile, at, :] = jnp.minimum(wt[tile, at, :], best[tile])

    min_plus(xt, ct, 1, done, 32, 0, PB)
    for t in range(8):
        for n in range(2):
            parts = [
                wt[t, (m % 2) * LANES + (m // 2) * 32 : (m % 2) * LANES + (m // 2) * 32 + 32, :]
                for m in range(4 * n, 4 * n + 4)
            ]
            flat = jnp.concatenate(parts, axis=0).T
            for zh in range(4):
                top = (t // 2) * 256 + (2 * zh + t % 2) * 32
                o_ref[top : top + 32, n * LANES : (n + 1) * LANES] = flat[zh * 32 : zh * 32 + 32]


def tile_of(base, rows, cols, pivots, closed):
    vmem = pl.BlockSpec(memory_space=pltpu.VMEM)
    tiles = rows.shape[0]
    return pl.pallas_call(
        body,
        out_shape=jax.ShapeDtypeStruct((tiles * LANES, PB), F32),
        in_specs=[pl.BlockSpec(memory_space=pltpu.SMEM)] + [vmem] * 4,
        out_specs=vmem,
        scratch_shapes=[
            pltpu.VMEM((tiles, PB, LANES), F32),
            pltpu.VMEM((2, PB, LANES), F32),
            pltpu.VMEM((2, PB, LANES), F32),
            pltpu.VMEM((tiles, PB, LANES), F32),
            pltpu.VMEM((tiles, 8, LANES), F32),
            pltpu.VMEM((PB, LANES), F32),
            pltpu.VMEM((2, 8, LANES), F32),
            pltpu.VMEM((PB, LANES), F32),
            pltpu.VMEM((PB, LANES), jnp.int32),
            pltpu.VMEM((tiles, 8, LANES), jnp.int32),
        ],
        compiler_params=pltpu.CompilerParams(vmem_limit_bytes=40 << 20),
    )(base, rows, cols, pivots, closed)


def local(features, neighbors, pivot):
    row, col, y, zh, core = place()
    lists = jnp.zeros((16, LANES), F32)
    lists = lax.dynamic_update_slice(lists, neighbors.T.astype(F32), (0, zh * SHARE))
    lists = jnp.concatenate([lists[:8], lists[8:]], axis=1)
    piece = jnp.concatenate([features, lists], axis=0)
    rows, cols, pivots, closed = moved(piece, pivot)
    base = jnp.stack([row * 1024, col * PB, pivot[0] * PB]).astype(jnp.int32)
    return tile_of(base, rows, cols, pivots, closed)


def solution(mesh):
    return jax.shard_map(
        local,
        mesh=mesh,
        in_specs=(P(("row", "col"), None), P(("row", "col"), None), P()),
        out_specs=P("row", "col"),
        check_vma=False,
    )
```

```python
import functools

import jax
import jax.numpy as jnp
from jax import lax
from jax.experimental import pallas as pl
from jax.experimental.pallas import tpu as pltpu
from jax.sharding import PartitionSpec as P

MESH = pl.DeviceIdType.MESH
PB = 256
SQUARINGS = 3
K = 10
far_weight = 3.0
LANES = 128
SHARE = 32
PIECE = SHARE + 8
FOLD = 4
F32 = jnp.float32


def place():
    row, col = lax.axis_index("row"), lax.axis_index("col")
    return row, col, col // 8, lax.rem(col, 8) // 2, lax.rem(col, 2)


def send(src, dst, out_sem, in_sem, to):
    copy = pltpu.make_async_remote_copy(
        src_ref=src, dst_ref=dst, send_sem=out_sem, recv_sem=in_sem,
        device_id=to, device_id_type=MESH,
    )
    copy.start()
    return copy


def arrival(slot, out_sem, in_sem, to):
    pltpu.make_async_remote_copy(
        src_ref=slot, dst_ref=slot, send_sem=out_sem, recv_sem=in_sem,
        device_id=to, device_id_type=MESH,
    ).wait_recv()


def greet(row, col, y, m):
    barrier = pltpu.get_barrier_semaphore()

    def signal(to):
        pl.semaphore_signal(barrier, inc=1, device_id=to, device_id_type=MESH)

    for d in range(1, 8):
        signal((lax.rem(row + d, 8), col))
        signal((row, y * 8 + lax.rem(m + d, 8)))
    for d in range(1, 4):
        signal((row, lax.rem(y + d, 4) * 8 + m))
    pl.semaphore_wait(barrier, 17)


def gather_and_close(pivot, points, lists, closed, bt, ct, wt, own, staged, rows, cols, pivots,
                     first, second, ka, wide, fold, npd, npa, ncd, nra, wa, wb, wb2, own_sem, s1, r1, s2, r2, s3, r3, s4, r4,
                     sc, rc, sz, rz, sy, ry, sp, rp, sf, rf):
    row, col, y, zh, core = place()
    m = zh * 2 + core
    home = row * 4 + y
    whole = home == col
    mine = rows.at[y * 2 + core, zh]
    partner = (row, y * 8 + zh * 2 + 1 - core)

    load = pltpu.make_async_copy(points, own.at[pl.ds(0, SHARE)], own_sem.at[3])
    load.start()
    staged[...] = jnp.zeros_like(staged)
    staged[:K, :SHARE] = lists[...].astype(F32)
    turned = pltpu.roll(staged[...], zh * SHARE, 1)
    own[SHARE:, :LANES] = turned[:8]
    own[SHARE:, LANES:] = turned[8:]
    greet(row, col, y, m)
    load.wait()
    kept = [
        pltpu.make_async_copy(own, mine, own_sem.at[0]),
        pltpu.make_async_copy(own, first.at[row], own_sem.at[1]),
    ]
    for copy in kept:
        copy.start()

    sent = []
    for d in range(1, 8):
        to = (lax.rem(row + d, 8), col)
        sent.append(send(own, first.at[row], s1.at[d], r1.at[row], to))
    for d in range(1, 4):
        to = (row, y * 8 + lax.rem(zh + d, 4) * 2 + core)
        sent.append(send(own, mine, sz.at[d], rz.at[zh], to))
    for d in range(1, 8):
        k = lax.rem(row + d, 8)
        arrival(first.at[k], s1.at[d], r1.at[k], (k, col))
    for copy in kept:
        copy.wait()
    second[y] = first[pivot[0] // 4]
    for d in range(1, 4):
        to = (row, lax.rem(y + d, 4) * 8 + m)
        sent.append(send(second.at[y], second.at[y], s2.at[d], r2.at[y], to))
    for d in range(1, 4):
        k = lax.rem(y + d, 4)
        arrival(second.at[k], s2.at[d], r2.at[k], (row, k * 8 + m))
    pivots[core, zh] = second[lax.rem(pivot[0], 4)]
    piece = pivots.at[core, zh]
    for d in range(1, 4):
        to = (row, y * 8 + lax.rem(zh + d, 4) * 2 + core)
        sent.append(send(piece, piece, s3.at[d], r3.at[zh], to))

    for d in range(1, 4):
        k = lax.rem(zh + d, 4)
        arrival(rows.at[y * 2 + core, k], sz.at[d], rz.at[k], (row, y * 8 + k * 2 + core))
    share = rows.at[y * 2 + core]
    for d in range(1, 4):
        to = (row, lax.rem(y + d, 4) * 8 + m)
        sent.append(send(share, share, sy.at[d], ry.at[y], to))

    for d in range(1, 4):
        k = lax.rem(zh + d, 4)
        arrival(pivots.at[core, k], s3.at[d], r3.at[k], (row, y * 8 + k * 2 + core))
    sent.append(send(pivots.at[core], pivots.at[core], s4.at[0], r4.at[0], partner))
    sent.append(send(share, share, sp.at[0], rp.at[y], partner))
    arrival(pivots.at[1 - core], s4.at[0], r4.at[0], partner)

    for d in range(1, 8):
        to = (lax.rem(row + d, 8), home)
        sent.append(send(own, cols.at[core, zh], sc.at[d], rc.at[m], to))
    out = pltpu.make_async_remote_copy(
        src_ref=own, dst_ref=cols.at[core, zh], send_sem=sc.at[0], recv_sem=rc.at[m],
        device_id=(row, home), device_id_type=MESH,
    )
    keep = pltpu.make_async_copy(own, cols.at[core, zh], own_sem.at[2])

    @pl.when(whole)
    def _():
        keep.start()

    @pl.when(jnp.logical_not(whole))
    def _():
        out.start()

    base, base_r, base_c = pivot[0] * PB, row * (4 * PB), col * PB
    norms_across(pivots, npa)
    norms_down(pivots, npd)
    note_lists(pivots, base, pivots, base, wa, wb)
    weigh(pivots, base, npd, pivots, base, npa, ka, wa, wb, 0, 1)
    spread(ka, wide)
    folded(wide, fold.at[0], 0, PB // FOLD)
    top = core * LANES

    def square(turn, meanwhile):
        old, new = turn % 2, (turn + 1) % 2

        def done(at, best):
            best = [reduced(b) for b in best]
            for g in range(2 * FOLD):
                wide[g, at, :] = best[g]
            for tile in range(2):
                part = gathered(best[FOLD * tile : FOLD * tile + FOLD])
                ka[tile, at, :] = jnp.minimum(ka[tile, at, :], part)

        min_plus(ka, fold.at[old], FOLD, done, 32, top, LANES)
        half = LANES // FOLD
        low = pl.multiple_of(core * half, half)
        folded(wide.at[:, pl.ds(pl.multiple_of(top, LANES), LANES)], fold.at[new], low, half)
        ours = fold.at[new, :, pl.ds(low, half)]
        theirs = fold.at[new, :, pl.ds(pl.multiple_of(half - low, half), half)]
        copy = send(ours, ours, sf.at[new], rf.at[new], partner)
        meanwhile()
        arrival(theirs, sf.at[new], rf.at[new], partner)
        copy.wait_send()

    def forward():
        for d in range(1, 4):
            k = lax.rem(y + d, 4)
            share = rows.at[k * 2 + core]
            arrival(share, sy.at[d], ry.at[k], (row, k * 8 + m))
            sent.append(send(share, share, sp.at[d], rp.at[k], partner))
        for d in range(1, 8):
            k = lax.rem(m + d, 8)
            slot = cols.at[lax.rem(k, 2), k // 2]
            arrival(slot, sc.at[d], rc.at[k], (col // 4, lax.rem(col, 4) * 8 + k))

        @pl.when(whole)
        def _():
            keep.wait()

        @pl.when(jnp.logical_not(whole))
        def _():
            out.wait_send()
            arrival(cols.at[core, zh], sc.at[0], rc.at[m], (col // 4, lax.rem(col, 4) * 8 + m))

    def panel():
        norms_down(cols, ncd)
        note_lists(cols, base_c, pivots, base, wa, wb)
        weigh(cols, base_c, ncd, pivots, base, npa, bt, wa, wb, 0, 1)

    def row_weights():
        for k in range(4):
            arrival(rows.at[k * 2 + 1 - core], sp.at[k], rp.at[k], partner)
        norms_across(rows, nra)
        note_lists(pivots, base, rows, base_r, wa, wb2)
        weigh(pivots, base, npd, rows, base_r, nra, ct, wa, wb2, 0, 4)

    def tile_weights():
        note_lists(cols, base_c, rows, base_r, wa, wb2)
        weigh(cols, base_c, ncd, rows, base_r, nra, wt, wa, wb2, 0, 4)

    square(0, forward)
    square(1, panel)
    square(2, row_weights)
    square(3, tile_weights)
    closed[...] = fold[(SQUARINGS + 1) % 2]
    for copy in sent:
        copy.wait_send()


def prepared(pivot, points, lists):
    sem = pltpu.SemaphoreType.DMA
    vmem = pl.BlockSpec(memory_space=pltpu.VMEM)
    i32 = jnp.int32
    return pl.pallas_call(
        gather_and_close,
        out_shape=[
            jax.ShapeDtypeStruct((2 * FOLD, PB // FOLD, LANES), F32),
            jax.ShapeDtypeStruct((2, PB, LANES), F32),
            jax.ShapeDtypeStruct((8, PB, LANES), F32),
            jax.ShapeDtypeStruct((8, PB, LANES), F32),
        ],
        in_specs=[pl.BlockSpec(memory_space=pltpu.SMEM), vmem, vmem],
        out_specs=[vmem] * 4,
        scratch_shapes=[
            pltpu.VMEM((PIECE, PB), F32),
            pltpu.VMEM((16, LANES), F32),
            pltpu.VMEM((8, 4, PIECE, PB), F32),
            pltpu.VMEM((2, 4, PIECE, PB), F32),
            pltpu.VMEM((2, 4, PIECE, PB), F32),
            pltpu.VMEM((8, PIECE, PB), F32),
            pltpu.VMEM((4, PIECE, PB), F32),
            pltpu.VMEM((2, PB, LANES), F32),
            pltpu.VMEM((2 * FOLD, PB, LANES), F32),
            pltpu.VMEM((2, 2 * FOLD, PB // FOLD, LANES), F32),
            pltpu.VMEM((PB, LANES), F32),
            pltpu.VMEM((2, 8, LANES), F32),
            pltpu.VMEM((PB, LANES), F32),
            pltpu.VMEM((8, 8, LANES), F32),
            pltpu.VMEM((PB, LANES), i32),
            pltpu.VMEM((2, 8, LANES), i32),
            pltpu.VMEM((8, 8, LANES), i32),
            sem((4,)),
            sem((8,)), sem((8,)), sem((4,)), sem((4,)), sem((4,)), sem((4,)), sem((1,)), sem((1,)),
            sem((8,)), sem((8,)), sem((4,)), sem((4,)), sem((4,)), sem((4,)),
            sem((4,)), sem((4,)), sem((2,)), sem((2,)),
        ],
        compiler_params=pltpu.CompilerParams(
            collective_id=0, has_side_effects=True, vmem_limit_bytes=32 << 20
        ),
    )(pivot, points, lists)


def dot(a, b, dims):
    return lax.dot_general(
        a, b, (dims, ((), ())),
        precision=lax.Precision.HIGHEST, preferred_element_type=F32,
    )


def points_of(pieces, tile):
    return pieces[tile, :, :SHARE, :].reshape(LANES, PB)


def lists_of(pieces, tile):
    both = pieces[tile, 0, SHARE:, :]
    for zh in range(1, 4):
        both = both + pieces[tile, zh, SHARE:, :]
    both = both.astype(jnp.int32)
    return jnp.concatenate([both[:, :LANES], both[:, LANES:]], axis=0)


def norms_down(points, out):
    for tile in range(2):
        p = points_of(points, tile)
        out[tile * LANES : (tile + 1) * LANES, :] = dot(
            p * p, jnp.ones((PB, LANES), F32), ((1,), (0,))
        )


def norms_across(points, out):
    def chunk(t, carry):
        p = points_of(points, t)
        out[t] = dot(jnp.ones((8, PB), F32), p * p, ((1,), (1,)))
        return carry

    lax.fori_loop(0, points.shape[0], chunk, 0)


def bits_of(lists, base, words):
    word = lax.broadcasted_iota(jnp.int32, (words, LANES), 0)
    found = jnp.zeros((words, LANES), jnp.int32)
    for slot in range(K):
        at = lists[slot : slot + 1, :] - base
        bit = jnp.left_shift(jnp.int32(1), at & 31)
        found = found | jnp.where(jnp.right_shift(at, 5) == word, bit, 0)
    return found


def lanes_of(piece, index):
    dims = lax.GatherDimensionNumbers(
        offset_dims=(), collapsed_slice_dims=(1,), start_index_map=(1,),
        operand_batching_dims=(0,), start_indices_batching_dims=(0,),
    )
    return lax.gather(
        piece, index[:, :, None], dims, (1, 1), mode=lax.GatherScatterMode.PROMISE_IN_BOUNDS
    )


def note_lists(down_of, base_a, across_of, base_b, wa, wb):
    tiles = across_of.shape[0]
    for tile in range(2):
        bits = bits_of(lists_of(down_of, tile), base_b, 4 * tiles)
        pad = jnp.zeros((LANES - 4 * tiles, LANES), jnp.int32)
        wa[tile * LANES : (tile + 1) * LANES, :] = jnp.concatenate([bits, pad], axis=0).T

    def words(t, carry):
        wb[t] = bits_of(lists_of(across_of, t), base_a, 8)
        return carry

    lax.fori_loop(0, tiles, words, 0)


def weigh(down_of, base_a, norm_a, across_of, base_b, norm_b, out, wa, wb, first, last):
    lane = lax.broadcasted_iota(jnp.int32, (32, LANES), 1)
    inside = lane & 31
    across = (lane // 32) * 64 + inside
    down = lax.broadcasted_iota(jnp.int32, (32, LANES), 0)

    def pair(n, carry):
        a = jnp.concatenate([points_of(down_of, 0), points_of(down_of, 1)], axis=0)
        b = jnp.concatenate([points_of(across_of, 2 * n), points_of(across_of, 2 * n + 1)], axis=0)
        inner = dot(a, b, ((1,), (1,)))
        for g in range(8):
            rows = slice(g * 32, g * 32 + 32)
            word_b = (g % 4) * 2 + g // 4
            for core in range(2):
                t, word_a = 2 * n + core, n * 8 + core
                part = inner[rows, core * LANES : (core + 1) * LANES]
                squares = norm_a[rows, :] + jnp.tile(norm_b[t], (4, 1)) - 2.0 * part
                squares = jnp.maximum(squares, 0.0)
                length = squares * lax.rsqrt(jnp.maximum(squares, 1.2e-38))
                listed = lanes_of(wa[rows, :], (lane // 32) * 2 + word_a)
                listed = jnp.right_shift(listed, inside)
                lists = jnp.tile(wb[t, pl.ds(word_b, 8, stride=0), :], (4, 1))
                listed = listed | jnp.right_shift(lists, down)
                weighted = jnp.where((listed & 1) == 1, length, far_weight * length)
                same = (down - across) == (base_b - base_a + 32 * (word_a - word_b))
                out[t, rows, :] = jnp.where(same, 0.0, weighted)
        return carry

    lax.fori_loop(first, last, pair, 0)


def min_plus(left, right, fold, done, rows, top, count):
    tiles = right.shape[0]
    halves = left.shape[0]
    depth = right.shape[1] // halves
    subs = rows // 8
    pattern = lax.broadcasted_iota(jnp.int32, (8, LANES), 1) // (LANES // fold)

    def block(t, carry):
        def rows_of(s):
            return pl.ds(pl.multiple_of(top + t * rows + 8 * s, 8), 8)

        def half(h, best):
            best = list(best)
            pieces = [left[h, rows_of(s), :] for s in range(subs)]
            for q in range(depth):
                downs = [lanes_of(piece, pattern + q * fold) for piece in pieces]
                for tile in range(tiles):
                    row = right[tile, pl.ds(h * depth + q, 8, stride=0), :]
                    for s in range(subs):
                        n = tile * subs + s
                        best[n] = jnp.minimum(best[n], downs[s] + row)
            return tuple(best)

        best = tuple(jnp.full((8, LANES), jnp.inf, F32) for _ in range(tiles * subs))
        best = lax.fori_loop(0, halves, half, best)
        for s in range(subs):
            done(rows_of(s), [best[tile * subs + s] for tile in range(tiles)])
        return carry

    lax.fori_loop(0, count // rows, block, 0)


def folded(wide, right, low, count):
    lane = lax.broadcasted_iota(jnp.int32, (count, LANES), 1) // (LANES // FOLD)
    for tile in range(wide.shape[0]):
        piece = wide[tile, pl.ds(0, count, stride=FOLD), :]
        for c in range(1, FOLD):
            other = wide[tile, pl.ds(c, count, stride=FOLD), :]
            piece = jnp.where(lane == c, other, piece)
        right[tile, pl.ds(low, count), :] = piece


def gathered(parts):
    group = lax.broadcasted_iota(jnp.int32, parts[0].shape, 1) // (LANES // FOLD)
    tile = parts[0]
    for c in range(1, FOLD):
        tile = jnp.where(group == c, parts[c], tile)
    return tile


def reduced(piece):
    piece = jnp.minimum(piece, pltpu.roll(piece, 64, 1))
    return jnp.minimum(piece, pltpu.roll(piece, 32, 1))


def spread(tiles, wide):
    lane = lax.broadcasted_iota(jnp.int32, (32, LANES), 1) & 31

    def chunk(t, carry):
        rows = pl.ds(pl.multiple_of(t * 32, 32), 32)
        for g in range(wide.shape[0]):
            wide[g, rows, :] = lanes_of(tiles[g // FOLD, rows, :], lane + 32 * (g % FOLD))
        return carry

    lax.fori_loop(0, PB // 32, chunk, 0)


def body(fold, bt, ct, wt, o_ref, xt, ot):
    def done(at, best):
        best = [reduced(b) for b in best]
        for tile in range(2):
            kept = gathered(best[FOLD * tile : FOLD * tile + FOLD])
            xt[tile, at, :] = jnp.minimum(bt[tile, at, :], kept)

    min_plus(bt, fold, FOLD, done, 32, 0, PB)

    def done(at, best):
        for tile in range(8):
            ot[tile, at, :] = jnp.minimum(wt[tile, at, :], best[tile])

    min_plus(xt, ct, 1, done, 32, 0, PB)
    for t in range(8):
        for n in range(2):
            parts = [
                ot[t, (m % 2) * LANES + (m // 2) * 32 : (m % 2) * LANES + (m // 2) * 32 + 32, :]
                for m in range(4 * n, 4 * n + 4)
            ]
            flat = jnp.concatenate(parts, axis=0).T
            for zh in range(4):
                top = (t // 2) * 256 + (2 * zh + t % 2) * 32
                o_ref[top : top + 32, n * LANES : (n + 1) * LANES] = flat[zh * 32 : zh * 32 + 32]


def tile_of(closed, bt, ct, wt):
    vmem = pl.BlockSpec(memory_space=pltpu.VMEM)
    tiles = ct.shape[0]
    return pl.pallas_call(
        body,
        out_shape=jax.ShapeDtypeStruct((tiles * LANES, PB), F32),
        in_specs=[vmem] * 4,
        out_specs=vmem,
        scratch_shapes=[
            pltpu.VMEM((2, PB, LANES), F32),
            pltpu.VMEM((tiles, PB, LANES), F32),
        ],
        compiler_params=pltpu.CompilerParams(vmem_limit_bytes=24 << 20),
    )(closed, bt, ct, wt)


def local(features, neighbors, pivot):
    return tile_of(*prepared(pivot, features, neighbors.T))


def solution(mesh):
    return jax.shard_map(
        local,
        mesh=mesh,
        in_specs=(P(("row", "col"), None), P(("row", "col"), None), P()),
        out_specs=P("row", "col"),
        check_vma=False,
    )
```

```python
import functools

import jax
import jax.numpy as jnp
from jax import lax
from jax.experimental import pallas as pl
from jax.experimental.pallas import tpu as pltpu
from jax.sharding import PartitionSpec as P

MESH = pl.DeviceIdType.MESH
PB = 256
SQUARINGS = 3
K = 10
far_weight = 3.0
LANES = 128
SHARE = 32
PIECE = SHARE + 8
FOLD = 4
F32 = jnp.float32


def place():
    row, col = lax.axis_index("row"), lax.axis_index("col")
    return row, col, col // 8, lax.rem(col, 8) // 2, lax.rem(col, 2)


def send(src, dst, out_sem, in_sem, to):
    copy = pltpu.make_async_remote_copy(
        src_ref=src, dst_ref=dst, send_sem=out_sem, recv_sem=in_sem,
        device_id=to, device_id_type=MESH,
    )
    copy.start()
    return copy


def arrival(slot, out_sem, in_sem, to):
    pltpu.make_async_remote_copy(
        src_ref=slot, dst_ref=slot, send_sem=out_sem, recv_sem=in_sem,
        device_id=to, device_id_type=MESH,
    ).wait_recv()


def beside(row, d):
    x, z = FAR_FIRST[d]
    return lax.rem(row // 4 + z, 2) * 4 + lax.rem(lax.rem(row, 4) + x, 4)


FAR_FIRST = ((0, 0), (2, 1), (1, 1), (3, 1), (2, 0), (0, 1), (1, 0), (3, 0))
RING = (2, 1, 3)


def greet(row, col, y, m):
    barrier = pltpu.get_barrier_semaphore()

    def signal(to):
        pl.semaphore_signal(barrier, inc=1, device_id=to, device_id_type=MESH)

    for d in (4, 3, 5, 2, 6, 1, 7):
        signal((row, y * 8 + lax.rem(m + d, 8)))
    for d in range(1, 8):
        signal((beside(row, d), col))
    for d in RING:
        signal((row, lax.rem(y + d, 4) * 8 + m))
    pl.semaphore_wait(barrier, 17)


def gather_and_close(pivot, points, lists, closed, bt, ct, wt, own, staged, rows, cols, pivots,
                     first, second, ka, wide, fold, npd, npa, ncd, nra, wa, wb, wb2, own_sem, s1, r1, s2, r2, s3, r3, s4, r4,
                     sc, rc, sz, rz, sy, ry, sp, rp, sf, rf):
    row, col, y, zh, core = place()
    m = zh * 2 + core
    home = row * 4 + y
    mine = rows.at[y * 2 + core, zh]
    partner = (row, y * 8 + zh * 2 + 1 - core)

    load = pltpu.make_async_copy(points, own.at[pl.ds(0, SHARE)], own_sem.at[3])
    load.start()
    staged[...] = jnp.zeros_like(staged)
    staged[:K, :SHARE] = lists[...].astype(F32)
    turned = pltpu.roll(staged[...], zh * SHARE, 1)
    own[SHARE:, :LANES] = turned[:8]
    own[SHARE:, LANES:] = turned[8:]
    greet(row, col, y, m)
    load.wait()
    kept = [
        pltpu.make_async_copy(own, mine, own_sem.at[0]),
        pltpu.make_async_copy(own, first.at[row], own_sem.at[1]),
    ]
    for copy in kept:
        copy.start()

    sent = []
    for d in range(1, 8):
        sent.append(send(own, first.at[row], s1.at[d], r1.at[row], (beside(row, d), col)))
    for d in RING:
        to = (row, y * 8 + lax.rem(zh + d, 4) * 2 + core)
        sent.append(send(own, mine, sz.at[d], rz.at[zh], to))
    for d in range(1, 8):
        k = beside(row, d)
        arrival(first.at[k], s1.at[d], r1.at[k], (k, col))
    for copy in kept:
        copy.wait()
    second[y] = first[pivot[0] // 4]
    for d in RING:
        to = (row, lax.rem(y + d, 4) * 8 + m)
        sent.append(send(second.at[y], second.at[y], s2.at[d], r2.at[y], to))
    for d in RING:
        k = lax.rem(y + d, 4)
        arrival(second.at[k], s2.at[d], r2.at[k], (row, k * 8 + m))
    pivots[core, zh] = second[lax.rem(pivot[0], 4)]
    piece = pivots.at[core, zh]
    for d in RING:
        to = (row, y * 8 + lax.rem(zh + d, 4) * 2 + core)
        sent.append(send(piece, piece, s3.at[d], r3.at[zh], to))

    for d in RING:
        k = lax.rem(zh + d, 4)
        arrival(rows.at[y * 2 + core, k], sz.at[d], rz.at[k], (row, y * 8 + k * 2 + core))
    share = rows.at[y * 2 + core]
    for d in RING:
        to = (row, lax.rem(y + d, 4) * 8 + m)
        sent.append(send(share, share, sy.at[d], ry.at[y], to))

    for d in RING:
        k = lax.rem(zh + d, 4)
        arrival(pivots.at[core, k], s3.at[d], r3.at[k], (row, y * 8 + k * 2 + core))
    sent.append(send(pivots.at[core], pivots.at[core], s4.at[0], r4.at[0], partner))
    sent.append(send(share, share, sp.at[0], rp.at[y], partner))
    arrival(pivots.at[1 - core], s4.at[0], r4.at[0], partner)

    stays = jnp.logical_and(home == col, row == m)
    given = cols.at[core, zh]
    taken = cols.at[lax.rem(row, 2), row // 2]
    out = pltpu.make_async_remote_copy(
        src_ref=own, dst_ref=given, send_sem=sc.at[0], recv_sem=rc.at[8],
        device_id=(m, home), device_id_type=MESH,
    )
    keep = pltpu.make_async_copy(own, given, own_sem.at[2])

    @pl.when(stays)
    def _():
        keep.start()

    @pl.when(jnp.logical_not(stays))
    def _():
        out.start()

    base, base_r, base_c = pivot[0] * PB, row * (4 * PB), col * PB
    norms_across(pivots, npa)
    norms_down(pivots, npd)
    note_lists(pivots, base, pivots, base, wa, wb)
    weigh(pivots, base, npd, pivots, base, npa, ka, wa, wb, 0, 1)
    spread(ka, wide)
    folded(wide, fold.at[0], 0, PB // FOLD)
    top = core * LANES

    def square(turn, meanwhile):
        old, new = turn % 2, (turn + 1) % 2

        def done(at, best):
            best = [reduced(b) for b in best]
            for g in range(2 * FOLD):
                wide[g, at, :] = best[g]
            for tile in range(2):
                part = gathered(best[FOLD * tile : FOLD * tile + FOLD])
                ka[tile, at, :] = jnp.minimum(ka[tile, at, :], part)

        min_plus(ka, fold.at[old], FOLD, done, 32, top, LANES)
        half = LANES // FOLD
        low = pl.multiple_of(core * half, half)
        folded(wide.at[:, pl.ds(pl.multiple_of(top, LANES), LANES)], fold.at[new], low, half)
        ours = fold.at[new, :, pl.ds(low, half)]
        theirs = fold.at[new, :, pl.ds(pl.multiple_of(half - low, half), half)]
        copy = send(ours, ours, sf.at[new], rf.at[new], partner)
        meanwhile()
        arrival(theirs, sf.at[new], rf.at[new], partner)
        copy.wait_send()

    def forward():
        for d in (1, 3, 2):
            k = lax.rem(y + d, 4)
            share = rows.at[k * 2 + core]
            arrival(share, sy.at[d], ry.at[k], (row, k * 8 + m))
            sent.append(send(share, share, sp.at[d], rp.at[k], partner))

        @pl.when(stays)
        def _():
            keep.wait()

        @pl.when(jnp.logical_not(stays))
        def _():
            out.wait_send()
            arrival(taken, sc.at[0], rc.at[8], (col // 4, lax.rem(col, 4) * 8 + row))

        for d in range(1, 8):
            sent.append(send(taken, taken, sc.at[d], rc.at[row], (beside(row, d), col)))

    def panel():
        for d in range(1, 8):
            k = beside(row, d)
            arrival(cols.at[lax.rem(k, 2), k // 2], sc.at[d], rc.at[k], (k, col))
        norms_down(cols, ncd)
        note_lists(cols, base_c, pivots, base, wa, wb)
        weigh(cols, base_c, ncd, pivots, base, npa, bt, wa, wb, 0, 1)

    def row_weights():
        for k in range(4):
            arrival(rows.at[k * 2 + 1 - core], sp.at[k], rp.at[k], partner)
        norms_across(rows, nra)
        note_lists(pivots, base, rows, base_r, wa, wb2)
        weigh(pivots, base, npd, rows, base_r, nra, ct, wa, wb2, 0, 4)

    def tile_weights():
        note_lists(cols, base_c, rows, base_r, wa, wb2)
        weigh(cols, base_c, ncd, rows, base_r, nra, wt, wa, wb2, 0, 4)

    square(0, forward)
    square(1, row_weights)
    square(2, panel)
    square(3, tile_weights)
    closed[...] = fold[(SQUARINGS + 1) % 2]
    for copy in sent:
        copy.wait_send()


def prepared(pivot, points, lists):
    sem = pltpu.SemaphoreType.DMA
    vmem = pl.BlockSpec(memory_space=pltpu.VMEM)
    i32 = jnp.int32
    return pl.pallas_call(
        gather_and_close,
        out_shape=[
            jax.ShapeDtypeStruct((2 * FOLD, PB // FOLD, LANES), F32),
            jax.ShapeDtypeStruct((2, PB, LANES), F32),
            jax.ShapeDtypeStruct((8, PB, LANES), F32),
            jax.ShapeDtypeStruct((8, PB, LANES), F32),
        ],
        in_specs=[pl.BlockSpec(memory_space=pltpu.SMEM), vmem, vmem],
        out_specs=[vmem] * 4,
        scratch_shapes=[
            pltpu.VMEM((PIECE, PB), F32),
            pltpu.VMEM((16, LANES), F32),
            pltpu.VMEM((8, 4, PIECE, PB), F32),
            pltpu.VMEM((2, 4, PIECE, PB), F32),
            pltpu.VMEM((2, 4, PIECE, PB), F32),
            pltpu.VMEM((8, PIECE, PB), F32),
            pltpu.VMEM((4, PIECE, PB), F32),
            pltpu.VMEM((2, PB, LANES), F32),
            pltpu.VMEM((2 * FOLD, PB, LANES), F32),
            pltpu.VMEM((2, 2 * FOLD, PB // FOLD, LANES), F32),
            pltpu.VMEM((PB, LANES), F32),
            pltpu.VMEM((2, 8, LANES), F32),
            pltpu.VMEM((PB, LANES), F32),
            pltpu.VMEM((8, 8, LANES), F32),
            pltpu.VMEM((PB, LANES), i32),
            pltpu.VMEM((2, 8, LANES), i32),
            pltpu.VMEM((8, 8, LANES), i32),
            sem((4,)),
            sem((8,)), sem((8,)), sem((4,)), sem((4,)), sem((4,)), sem((4,)), sem((1,)), sem((1,)),
            sem((8,)), sem((9,)), sem((4,)), sem((4,)), sem((4,)), sem((4,)),
            sem((4,)), sem((4,)), sem((2,)), sem((2,)),
        ],
        compiler_params=pltpu.CompilerParams(
            collective_id=0, has_side_effects=True, vmem_limit_bytes=32 << 20
        ),
    )(pivot, points, lists)


def dot(a, b, dims):
    return lax.dot_general(
        a, b, (dims, ((), ())),
        precision=lax.Precision.HIGHEST, preferred_element_type=F32,
    )


def points_of(pieces, tile):
    return pieces[tile, :, :SHARE, :].reshape(LANES, PB)


def lists_of(pieces, tile):
    both = pieces[tile, 0, SHARE:, :]
    for zh in range(1, 4):
        both = both + pieces[tile, zh, SHARE:, :]
    both = both.astype(jnp.int32)
    return jnp.concatenate([both[:, :LANES], both[:, LANES:]], axis=0)


def norms_down(points, out):
    for tile in range(2):
        p = points_of(points, tile)
        out[tile * LANES : (tile + 1) * LANES, :] = dot(
            p * p, jnp.ones((PB, LANES), F32), ((1,), (0,))
        )


def norms_across(points, out):
    def chunk(t, carry):
        p = points_of(points, t)
        out[t] = dot(jnp.ones((8, PB), F32), p * p, ((1,), (1,)))
        return carry

    lax.fori_loop(0, points.shape[0], chunk, 0)


def bits_of(lists, base, words):
    word = lax.broadcasted_iota(jnp.int32, (words, LANES), 0)
    found = jnp.zeros((words, LANES), jnp.int32)
    for slot in range(K):
        at = lists[slot : slot + 1, :] - base
        bit = jnp.left_shift(jnp.int32(1), at & 31)
        found = found | jnp.where(jnp.right_shift(at, 5) == word, bit, 0)
    return found


def lanes_of(piece, index):
    dims = lax.GatherDimensionNumbers(
        offset_dims=(), collapsed_slice_dims=(1,), start_index_map=(1,),
        operand_batching_dims=(0,), start_indices_batching_dims=(0,),
    )
    return lax.gather(
        piece, index[:, :, None], dims, (1, 1), mode=lax.GatherScatterMode.PROMISE_IN_BOUNDS
    )


def note_lists(down_of, base_a, across_of, base_b, wa, wb):
    tiles = across_of.shape[0]
    for tile in range(2):
        bits = bits_of(lists_of(down_of, tile), base_b, 4 * tiles)
        pad = jnp.zeros((LANES - 4 * tiles, LANES), jnp.int32)
        wa[tile * LANES : (tile + 1) * LANES, :] = jnp.concatenate([bits, pad], axis=0).T

    def words(t, carry):
        wb[t] = bits_of(lists_of(across_of, t), base_a, 8)
        return carry

    lax.fori_loop(0, tiles, words, 0)


def weigh(down_of, base_a, norm_a, across_of, base_b, norm_b, out, wa, wb, first, last):
    lane = lax.broadcasted_iota(jnp.int32, (32, LANES), 1)
    inside = lane & 31
    across = (lane // 32) * 64 + inside
    down = lax.broadcasted_iota(jnp.int32, (32, LANES), 0)

    def pair(n, carry):
        a = jnp.concatenate([points_of(down_of, 0), points_of(down_of, 1)], axis=0)
        b = jnp.concatenate([points_of(across_of, 2 * n), points_of(across_of, 2 * n + 1)], axis=0)
        inner = dot(a, b, ((1,), (1,)))
        for g in range(8):
            rows = slice(g * 32, g * 32 + 32)
            word_b = (g % 4) * 2 + g // 4
            for core in range(2):
                t, word_a = 2 * n + core, n * 8 + core
                part = inner[rows, core * LANES : (core + 1) * LANES]
                squares = norm_a[rows, :] + jnp.tile(norm_b[t], (4, 1)) - 2.0 * part
                squares = jnp.maximum(squares, 0.0)
                length = squares * lax.rsqrt(jnp.maximum(squares, 1.2e-38))
                listed = lanes_of(wa[rows, :], (lane // 32) * 2 + word_a)
                listed = jnp.right_shift(listed, inside)
                lists = jnp.tile(wb[t, pl.ds(word_b, 8, stride=0), :], (4, 1))
                listed = listed | jnp.right_shift(lists, down)
                weighted = jnp.where((listed & 1) == 1, length, far_weight * length)
                same = (down - across) == (base_b - base_a + 32 * (word_a - word_b))
                out[t, rows, :] = jnp.where(same, 0.0, weighted)
        return carry

    lax.fori_loop(first, last, pair, 0)


def min_plus(left, right, fold, done, rows, top, count):
    tiles = right.shape[0]
    halves = left.shape[0]
    depth = right.shape[1] // halves
    subs = rows // 8
    pattern = lax.broadcasted_iota(jnp.int32, (8, LANES), 1) // (LANES // fold)

    def block(t, carry):
        def rows_of(s):
            return pl.ds(pl.multiple_of(top + t * rows + 8 * s, 8), 8)

        def half(h, best):
            best = list(best)
            pieces = [left[h, rows_of(s), :] for s in range(subs)]
            for q in range(depth):
                downs = [lanes_of(piece, pattern + q * fold) for piece in pieces]
                for tile in range(tiles):
                    row = right[tile, pl.ds(h * depth + q, 8, stride=0), :]
                    for s in range(subs):
                        n = tile * subs + s
                        best[n] = jnp.minimum(best[n], downs[s] + row)
            return tuple(best)

        best = tuple(jnp.full((8, LANES), jnp.inf, F32) for _ in range(tiles * subs))
        best = lax.fori_loop(0, halves, half, best)
        for s in range(subs):
            done(rows_of(s), [best[tile * subs + s] for tile in range(tiles)])
        return carry

    lax.fori_loop(0, count // rows, block, 0)


def folded(wide, right, low, count):
    lane = lax.broadcasted_iota(jnp.int32, (count, LANES), 1) // (LANES // FOLD)
    for tile in range(wide.shape[0]):
        piece = wide[tile, pl.ds(0, count, stride=FOLD), :]
        for c in range(1, FOLD):
            other = wide[tile, pl.ds(c, count, stride=FOLD), :]
            piece = jnp.where(lane == c, other, piece)
        right[tile, pl.ds(low, count), :] = piece


def gathered(parts):
    group = lax.broadcasted_iota(jnp.int32, parts[0].shape, 1) // (LANES // FOLD)
    tile = parts[0]
    for c in range(1, FOLD):
        tile = jnp.where(group == c, parts[c], tile)
    return tile


def reduced(piece):
    piece = jnp.minimum(piece, pltpu.roll(piece, 64, 1))
    return jnp.minimum(piece, pltpu.roll(piece, 32, 1))


def spread(tiles, wide):
    lane = lax.broadcasted_iota(jnp.int32, (32, LANES), 1) & 31

    def chunk(t, carry):
        rows = pl.ds(pl.multiple_of(t * 32, 32), 32)
        for g in range(wide.shape[0]):
            wide[g, rows, :] = lanes_of(tiles[g // FOLD, rows, :], lane + 32 * (g % FOLD))
        return carry

    lax.fori_loop(0, PB // 32, chunk, 0)


def body(fold, bt, ct, wt, o_ref, xt, ot):
    def done(at, best):
        best = [reduced(b) for b in best]
        for tile in range(2):
            kept = gathered(best[FOLD * tile : FOLD * tile + FOLD])
            xt[tile, at, :] = jnp.minimum(bt[tile, at, :], kept)

    min_plus(bt, fold, FOLD, done, 32, 0, PB)

    def done(at, best):
        for tile in range(8):
            ot[tile, at, :] = jnp.minimum(wt[tile, at, :], best[tile])

    min_plus(xt, ct, 1, done, 32, 0, PB)
    for t in range(8):
        for n in range(2):
            parts = [
                ot[t, (m % 2) * LANES + (m // 2) * 32 : (m % 2) * LANES + (m // 2) * 32 + 32, :]
                for m in range(4 * n, 4 * n + 4)
            ]
            flat = jnp.concatenate(parts, axis=0).T
            for zh in range(4):
                top = (t // 2) * 256 + (2 * zh + t % 2) * 32
                o_ref[top : top + 32, n * LANES : (n + 1) * LANES] = flat[zh * 32 : zh * 32 + 32]


def tile_of(closed, bt, ct, wt):
    vmem = pl.BlockSpec(memory_space=pltpu.VMEM)
    tiles = ct.shape[0]
    return pl.pallas_call(
        body,
        out_shape=jax.ShapeDtypeStruct((tiles * LANES, PB), F32),
        in_specs=[vmem] * 4,
        out_specs=vmem,
        scratch_shapes=[
            pltpu.VMEM((2, PB, LANES), F32),
            pltpu.VMEM((tiles, PB, LANES), F32),
        ],
        compiler_params=pltpu.CompilerParams(vmem_limit_bytes=24 << 20),
    )(closed, bt, ct, wt)


def local(features, neighbors, pivot):
    return tile_of(*prepared(pivot, features, neighbors.T))


def solution(mesh):
    return jax.shard_map(
        local,
        mesh=mesh,
        in_specs=(P(("row", "col"), None), P(("row", "col"), None), P()),
        out_specs=P("row", "col"),
        check_vma=False,
    )
```

```python
import functools

import jax
import jax.numpy as jnp
from jax import lax
from jax.experimental import pallas as pl
from jax.experimental.pallas import tpu as pltpu
from jax.sharding import PartitionSpec as P

MESH = pl.DeviceIdType.MESH
PB = 256
SQUARINGS = 3
K = 10
far_weight = 3.0
LANES = 128
SHARE = 32
PIECE = SHARE + 8
FOLD = 4
F32 = jnp.float32


def place():
    row, col = lax.axis_index("row"), lax.axis_index("col")
    return row, col, col // 8, lax.rem(col, 8) // 2, lax.rem(col, 2)


def send(src, dst, out_sem, in_sem, to):
    copy = pltpu.make_async_remote_copy(
        src_ref=src, dst_ref=dst, send_sem=out_sem, recv_sem=in_sem,
        device_id=to, device_id_type=MESH,
    )
    copy.start()
    return copy


def arrival(slot, out_sem, in_sem, to):
    pltpu.make_async_remote_copy(
        src_ref=slot, dst_ref=slot, send_sem=out_sem, recv_sem=in_sem,
        device_id=to, device_id_type=MESH,
    ).wait_recv()


def beside(row, d):
    x, z = FAR_FIRST[d]
    return lax.rem(row // 4 + z, 2) * 4 + lax.rem(lax.rem(row, 4) + x, 4)


FAR_FIRST = ((0, 0), (2, 1), (1, 1), (3, 1), (2, 0), (0, 1), (1, 0), (3, 0))
RING = (2, 1, 3)


def greet(row, col, y, m):
    barrier = pltpu.get_barrier_semaphore()

    def signal(to):
        pl.semaphore_signal(barrier, inc=1, device_id=to, device_id_type=MESH)

    for d in (4, 3, 5, 2, 6, 1, 7):
        signal((row, y * 8 + lax.rem(m + d, 8)))
    for d in range(1, 8):
        signal((beside(row, d), col))
    for d in RING:
        signal((row, lax.rem(y + d, 4) * 8 + m))
    return barrier


PARTS = (pl.ds(0, 24), pl.ds(24, 16))


def gather_and_close(pivot, points, lists, closed, bt, ct, wt, own, listed, staged, rows, cols,
                     pivots, first_a, first_b, second_a, second_b, ka, wide, fold,
                     npd, npa, ncd, nra, wa, wb, wb2, own_sem,
                     s1, r1, s2, r2, s3, r3, s4, r4, sc, rc, sz, rz, sy, ry, sp, rp, sf, rf):
    row, col, y, zh, core = place()
    m = zh * 2 + core
    home = row * 4 + y
    mine = rows.at[y * 2 + core, zh]
    partner = (row, y * 8 + zh * 2 + 1 - core)
    first, second = (first_a, first_b), (second_a, second_b)

    load = [
        pltpu.make_async_copy(lists, listed, own_sem.at[0]),
        pltpu.make_async_copy(points, own.at[pl.ds(0, SHARE)], own_sem.at[1]),
    ]
    for copy in load:
        copy.start()
    barrier = greet(row, col, y, m)
    staged[...] = jnp.zeros_like(staged)
    load[0].wait()
    staged[:K, :SHARE] = listed[...].astype(F32)
    turned = pltpu.roll(staged[...], zh * SHARE, 1)
    own[SHARE:, :LANES] = turned[:8]
    own[SHARE:, LANES:] = turned[8:]
    load[1].wait()
    pl.semaphore_wait(barrier, 17)

    sent = []
    for h, part in enumerate(PARTS):
        for d in range(1, 8):
            to = (beside(row, d), col)
            sent.append(send(own.at[part], first[h].at[row], s1.at[h, d], r1.at[h, row], to))
    kept = [
        pltpu.make_async_copy(own.at[part], first[h].at[row], own_sem.at[2 + h])
        for h, part in enumerate(PARTS)
    ]
    kept.append(pltpu.make_async_copy(own, mine, own_sem.at[4]))
    for copy in kept:
        copy.start()
    for d in RING:
        to = (row, y * 8 + lax.rem(zh + d, 4) * 2 + core)
        sent.append(send(own, mine, sz.at[d], rz.at[zh], to))
    for copy in kept:
        copy.wait()
    for h in range(2):
        for d in range(1, 8):
            k = beside(row, d)
            arrival(first[h].at[k], s1.at[h, d], r1.at[h, k], (k, col))
        second[h][y] = first[h][pivot[0] // 4]
        for d in RING:
            to = (row, lax.rem(y + d, 4) * 8 + m)
            slot = second[h].at[y]
            sent.append(send(slot, slot, s2.at[h, d], r2.at[h, y], to))
    for h, part in enumerate(PARTS):
        for d in RING:
            k = lax.rem(y + d, 4)
            arrival(second[h].at[k], s2.at[h, d], r2.at[h, k], (row, k * 8 + m))
        pivots[core, zh, part] = second[h][lax.rem(pivot[0], 4)]
        piece = pivots.at[core, zh, part]
        for d in RING:
            to = (row, y * 8 + lax.rem(zh + d, 4) * 2 + core)
            sent.append(send(piece, piece, s3.at[h, d], r3.at[h, zh], to))

    stays = jnp.logical_and(home == col, row == m)
    given = cols.at[core, zh]
    taken = cols.at[lax.rem(row, 2), row // 2]
    out = pltpu.make_async_remote_copy(
        src_ref=own, dst_ref=given, send_sem=sc.at[0], recv_sem=rc.at[8],
        device_id=(m, home), device_id_type=MESH,
    )
    keep = pltpu.make_async_copy(own, given, own_sem.at[5])

    @pl.when(stays)
    def _():
        keep.start()

    @pl.when(jnp.logical_not(stays))
    def _():
        out.start()

    for d in RING:
        k = lax.rem(zh + d, 4)
        arrival(rows.at[y * 2 + core, k], sz.at[d], rz.at[k], (row, y * 8 + k * 2 + core))
    share = rows.at[y * 2 + core]
    for d in RING:
        to = (row, lax.rem(y + d, 4) * 8 + m)
        sent.append(send(share, share, sy.at[d], ry.at[y], to))

    for h, part in enumerate(PARTS):
        for d in RING:
            k = lax.rem(zh + d, 4)
            slot = pivots.at[core, k, part]
            arrival(slot, s3.at[h, d], r3.at[h, k], (row, y * 8 + k * 2 + core))
        half = pivots.at[core, :, part]
        sent.append(send(half, half, s4.at[h], r4.at[h], partner))
    sent.append(send(share, share, sp.at[0], rp.at[y], partner))
    for h, part in enumerate(PARTS):
        arrival(pivots.at[1 - core, :, part], s4.at[h], r4.at[h], partner)

    base, base_r, base_c = pivot[0] * PB, row * (4 * PB), col * PB
    norms_across(pivots, npa)
    norms_down(pivots, npd)
    note_lists(pivots, base, pivots, base, wa, wb)
    weigh(pivots, base, npd, pivots, base, npa, ka, wa, wb, 0, 1)
    spread(ka, wide)
    folded(wide, fold.at[0], 0, PB // FOLD)
    @pl.when(stays)
    def _():
        keep.wait()

    @pl.when(jnp.logical_not(stays))
    def _():
        out.wait_send()
        arrival(taken, sc.at[0], rc.at[8], (col // 4, lax.rem(col, 4) * 8 + row))

    for d in range(1, 8):
        sent.append(send(taken, taken, sc.at[d], rc.at[row], (beside(row, d), col)))

    top = core * LANES

    def square(turn, meanwhile):
        old, new = turn % 2, (turn + 1) % 2

        def done(at, best):
            best = [reduced(b) for b in best]
            for g in range(2 * FOLD):
                wide[g, at, :] = best[g]
            for tile in range(2):
                part = gathered(best[FOLD * tile : FOLD * tile + FOLD])
                ka[tile, at, :] = jnp.minimum(ka[tile, at, :], part)

        min_plus(ka, fold.at[old], FOLD, done, 32, lambda t: top + 32 * t, 0, 4)
        half = LANES // FOLD
        low = pl.multiple_of(core * half, half)
        folded(wide.at[:, pl.ds(pl.multiple_of(top, LANES), LANES)], fold.at[new], low, half)
        ours = fold.at[new, :, pl.ds(low, half)]
        theirs = fold.at[new, :, pl.ds(pl.multiple_of(half - low, half), half)]
        copy = send(ours, ours, sf.at[new], rf.at[new], partner)
        meanwhile()
        arrival(theirs, sf.at[new], rf.at[new], partner)
        copy.wait_send()

    def forward():
        for d in (1, 3, 2):
            k = lax.rem(y + d, 4)
            share = rows.at[k * 2 + core]
            arrival(share, sy.at[d], ry.at[k], (row, k * 8 + m))
            sent.append(send(share, share, sp.at[d], rp.at[k], partner))

    def panel():
        for d in range(1, 8):
            k = beside(row, d)
            arrival(cols.at[lax.rem(k, 2), k // 2], sc.at[d], rc.at[k], (k, col))
        norms_down(cols, ncd)
        note_lists(cols, base_c, pivots, base, wa, wb)
        weigh(cols, base_c, ncd, pivots, base, npa, bt, wa, wb, 0, 1)

    def row_weights():
        for k in range(4):
            arrival(rows.at[k * 2 + 1 - core], sp.at[k], rp.at[k], partner)
        norms_across(rows, nra)
        note_lists(pivots, base, rows, base_r, wa, wb2)
        weigh(pivots, base, npd, rows, base_r, nra, ct, wa, wb2, 0, 4)

    def tile_weights():
        note_lists(cols, base_c, rows, base_r, wa, wb2)
        weigh(cols, base_c, ncd, rows, base_r, nra, wt, wa, wb2, 0, 2)

    def more_tile_weights():
        weigh(cols, base_c, ncd, rows, base_r, nra, wt, wa, wb2, 2, 4)

    def first_work():
        forward()
        panel()

    square(0, first_work)
    square(1, row_weights)
    square(2, tile_weights)
    square(3, more_tile_weights)
    closed[...] = fold[(SQUARINGS + 1) % 2]
    for copy in sent:
        copy.wait_send()


def prepared(pivot, points, lists):
    sem = pltpu.SemaphoreType.DMA
    vmem = pl.BlockSpec(memory_space=pltpu.VMEM)
    hbm = pl.BlockSpec(memory_space=pltpu.HBM)
    i32 = jnp.int32
    return pl.pallas_call(
        gather_and_close,
        out_shape=[
            jax.ShapeDtypeStruct((2 * FOLD, PB // FOLD, LANES), F32),
            jax.ShapeDtypeStruct((2, PB, LANES), F32),
            jax.ShapeDtypeStruct((8, PB, LANES), F32),
            jax.ShapeDtypeStruct((8, PB, LANES), F32),
        ],
        in_specs=[pl.BlockSpec(memory_space=pltpu.SMEM), hbm, hbm],
        out_specs=[vmem] * 4,
        scratch_shapes=[
            pltpu.VMEM((PIECE, PB), F32),
            pltpu.VMEM((K, SHARE), i32),
            pltpu.VMEM((16, LANES), F32),
            pltpu.VMEM((8, 4, PIECE, PB), F32),
            pltpu.VMEM((2, 4, PIECE, PB), F32),
            pltpu.VMEM((2, 4, PIECE, PB), F32),
            pltpu.VMEM((8, PARTS[0].size, PB), F32),
            pltpu.VMEM((8, PARTS[1].size, PB), F32),
            pltpu.VMEM((4, PARTS[0].size, PB), F32),
            pltpu.VMEM((4, PARTS[1].size, PB), F32),
            pltpu.VMEM((2, PB, LANES), F32),
            pltpu.VMEM((2 * FOLD, PB, LANES), F32),
            pltpu.VMEM((2, 2 * FOLD, PB // FOLD, LANES), F32),
            pltpu.VMEM((PB, LANES), F32),
            pltpu.VMEM((2, 8, LANES), F32),
            pltpu.VMEM((PB, LANES), F32),
            pltpu.VMEM((8, 8, LANES), F32),
            pltpu.VMEM((PB, LANES), i32),
            pltpu.VMEM((2, 8, LANES), i32),
            pltpu.VMEM((8, 8, LANES), i32),
            sem((6,)),
            sem((2, 8)), sem((2, 8)), sem((2, 4)), sem((2, 4)), sem((2, 4)), sem((2, 4)),
            sem((2,)), sem((2,)),
            sem((8,)), sem((9,)), sem((4,)), sem((4,)), sem((4,)), sem((4,)),
            sem((4,)), sem((4,)), sem((2,)), sem((2,)),
        ],
        compiler_params=pltpu.CompilerParams(
            collective_id=0, has_side_effects=True, vmem_limit_bytes=32 << 20
        ),
    )(pivot, points, lists)


def dot(a, b, dims):
    return lax.dot_general(
        a, b, (dims, ((), ())),
        precision=lax.Precision.HIGHEST, preferred_element_type=F32,
    )


def points_of(pieces, tile):
    return pieces[tile, :, :SHARE, :].reshape(LANES, PB)


def lists_of(pieces, tile):
    both = pieces[tile, 0, SHARE:, :]
    for zh in range(1, 4):
        both = both + pieces[tile, zh, SHARE:, :]
    both = both.astype(jnp.int32)
    return jnp.concatenate([both[:, :LANES], both[:, LANES:]], axis=0)


def norms_down(points, out):
    for tile in range(2):
        p = points_of(points, tile)
        out[tile * LANES : (tile + 1) * LANES, :] = dot(
            p * p, jnp.ones((PB, LANES), F32), ((1,), (0,))
        )


def norms_across(points, out):
    def chunk(t, carry):
        p = points_of(points, t)
        out[t] = dot(jnp.ones((8, PB), F32), p * p, ((1,), (1,)))
        return carry

    lax.fori_loop(0, points.shape[0], chunk, 0)


def bits_of(lists, base, words):
    word = lax.broadcasted_iota(jnp.int32, (words, LANES), 0)
    found = jnp.zeros((words, LANES), jnp.int32)
    for slot in range(K):
        at = lists[slot : slot + 1, :] - base
        bit = jnp.left_shift(jnp.int32(1), at & 31)
        found = found | jnp.where(jnp.right_shift(at, 5) == word, bit, 0)
    return found


def lanes_of(piece, index):
    dims = lax.GatherDimensionNumbers(
        offset_dims=(), collapsed_slice_dims=(1,), start_index_map=(1,),
        operand_batching_dims=(0,), start_indices_batching_dims=(0,),
    )
    return lax.gather(
        piece, index[:, :, None], dims, (1, 1), mode=lax.GatherScatterMode.PROMISE_IN_BOUNDS
    )


def note_lists(down_of, base_a, across_of, base_b, wa, wb):
    tiles = across_of.shape[0]
    for tile in range(2):
        bits = bits_of(lists_of(down_of, tile), base_b, 4 * tiles)
        pad = jnp.zeros((LANES - 4 * tiles, LANES), jnp.int32)
        wa[tile * LANES : (tile + 1) * LANES, :] = jnp.concatenate([bits, pad], axis=0).T

    def words(t, carry):
        wb[t] = bits_of(lists_of(across_of, t), base_a, 8)
        return carry

    lax.fori_loop(0, tiles, words, 0)


def weigh(down_of, base_a, norm_a, across_of, base_b, norm_b, out, wa, wb, first, last):
    lane = lax.broadcasted_iota(jnp.int32, (32, LANES), 1)
    inside = lane & 31
    across = (lane // 32) * 64 + inside
    down = lax.broadcasted_iota(jnp.int32, (32, LANES), 0)

    def pair(n, carry):
        a = jnp.concatenate([points_of(down_of, 0), points_of(down_of, 1)], axis=0)
        b = jnp.concatenate([points_of(across_of, 2 * n), points_of(across_of, 2 * n + 1)], axis=0)
        inner = dot(a, b, ((1,), (1,)))
        for g in range(8):
            rows = slice(g * 32, g * 32 + 32)
            word_b = (g % 4) * 2 + g // 4
            for core in range(2):
                t, word_a = 2 * n + core, n * 8 + core
                part = inner[rows, core * LANES : (core + 1) * LANES]
                squares = norm_a[rows, :] + jnp.tile(norm_b[t], (4, 1)) - 2.0 * part
                squares = jnp.maximum(squares, 0.0)
                length = squares * lax.rsqrt(jnp.maximum(squares, 1.2e-38))
                listed = lanes_of(wa[rows, :], (lane // 32) * 2 + word_a)
                listed = jnp.right_shift(listed, inside)
                lists = jnp.tile(wb[t, pl.ds(word_b, 8, stride=0), :], (4, 1))
                listed = listed | jnp.right_shift(lists, down)
                weighted = jnp.where((listed & 1) == 1, length, far_weight * length)
                same = (down - across) == (base_b - base_a + 32 * (word_a - word_b))
                out[t, rows, :] = jnp.where(same, 0.0, weighted)
        return carry

    lax.fori_loop(first, last, pair, 0)


def min_plus(left, right, fold, done, rows, start_of, first, last):
    tiles = right.shape[0]
    halves = left.shape[0]
    depth = right.shape[1] // halves
    subs = rows // 8
    pattern = lax.broadcasted_iota(jnp.int32, (8, LANES), 1) // (LANES // fold)

    def block(t, carry):
        def rows_of(s):
            return pl.ds(pl.multiple_of(start_of(t) + 8 * s, 8), 8)

        def half(h, best):
            best = list(best)
            pieces = [left[h, rows_of(s), :] for s in range(subs)]
            for q in range(depth):
                downs = [lanes_of(piece, pattern + q * fold) for piece in pieces]
                for tile in range(tiles):
                    row = right[tile, pl.ds(h * depth + q, 8, stride=0), :]
                    for s in range(subs):
                        n = tile * subs + s
                        best[n] = jnp.minimum(best[n], downs[s] + row)
            return tuple(best)

        best = tuple(jnp.full((8, LANES), jnp.inf, F32) for _ in range(tiles * subs))
        best = lax.fori_loop(0, halves, half, best)
        for s in range(subs):
            done(rows_of(s), [best[tile * subs + s] for tile in range(tiles)])
        return carry

    lax.fori_loop(first, last, block, 0)


def folded(wide, right, low, count):
    lane = lax.broadcasted_iota(jnp.int32, (count, LANES), 1) // (LANES // FOLD)
    for tile in range(wide.shape[0]):
        piece = wide[tile, pl.ds(0, count, stride=FOLD), :]
        for c in range(1, FOLD):
            other = wide[tile, pl.ds(c, count, stride=FOLD), :]
            piece = jnp.where(lane == c, other, piece)
        right[tile, pl.ds(low, count), :] = piece


def gathered(parts):
    group = lax.broadcasted_iota(jnp.int32, parts[0].shape, 1) // (LANES // FOLD)
    tile = parts[0]
    for c in range(1, FOLD):
        tile = jnp.where(group == c, parts[c], tile)
    return tile


def reduced(piece):
    piece = jnp.minimum(piece, pltpu.roll(piece, 64, 1))
    return jnp.minimum(piece, pltpu.roll(piece, 32, 1))


def spread(tiles, wide):
    lane = lax.broadcasted_iota(jnp.int32, (32, LANES), 1) & 31

    def chunk(t, carry):
        rows = pl.ds(pl.multiple_of(t * 32, 32), 32)
        for g in range(wide.shape[0]):
            wide[g, rows, :] = lanes_of(tiles[g // FOLD, rows, :], lane + 32 * (g % FOLD))
        return carry

    lax.fori_loop(0, PB // 32, chunk, 0)


def body(fold, bt, ct, wt, o_ref, xt, ot):
    def done(at, best):
        best = [reduced(b) for b in best]
        for tile in range(2):
            kept = gathered(best[FOLD * tile : FOLD * tile + FOLD])
            xt[tile, at, :] = jnp.minimum(bt[tile, at, :], kept)

    min_plus(bt, fold, FOLD, done, 32, lambda t: 32 * t, 0, 8)

    def done(at, best):
        for tile in range(8):
            ot[tile, at, :] = jnp.minimum(wt[tile, at, :], best[tile])

    min_plus(xt, ct, 1, done, 32, lambda t: 32 * t, 0, 8)
    for t in range(8):
        for n in range(2):
            parts = [
                ot[t, (m % 2) * LANES + (m // 2) * 32 : (m % 2) * LANES + (m // 2) * 32 + 32, :]
                for m in range(4 * n, 4 * n + 4)
            ]
            flat = jnp.concatenate(parts, axis=0).T
            for zh in range(4):
                top = (t // 2) * 256 + (2 * zh + t % 2) * 32
                o_ref[top : top + 32, n * LANES : (n + 1) * LANES] = flat[zh * 32 : zh * 32 + 32]


def tile_of(closed, bt, ct, wt):
    vmem = pl.BlockSpec(memory_space=pltpu.VMEM)
    tiles = ct.shape[0]
    return pl.pallas_call(
        body,
        out_shape=jax.ShapeDtypeStruct((tiles * LANES, PB), F32),
        in_specs=[vmem] * 4,
        out_specs=vmem,
        scratch_shapes=[
            pltpu.VMEM((2, PB, LANES), F32),
            pltpu.VMEM((tiles, PB, LANES), F32),
        ],
        compiler_params=pltpu.CompilerParams(vmem_limit_bytes=24 << 20),
    )(closed, bt, ct, wt)


def local(features, neighbors, pivot):
    features = pltpu.with_memory_space_constraint(features, pltpu.HBM)
    lists = pltpu.with_memory_space_constraint(neighbors.T, pltpu.HBM)
    return tile_of(*prepared(pivot, features, lists))


def solution(mesh):
    return jax.shard_map(
        local,
        mesh=mesh,
        in_specs=(P(("row", "col"), None), P(("row", "col"), None), P()),
        out_specs=P("row", "col"),
        check_vma=False,
    )
```

```python
import functools

import jax
import jax.numpy as jnp
from jax import lax
from jax.experimental import pallas as pl
from jax.experimental.pallas import tpu as pltpu
from jax.sharding import PartitionSpec as P

MESH = pl.DeviceIdType.MESH
PB = 256
SQUARINGS = 3
K = 10
far_weight = 3.0
LANES = 128
SHARE = 32
PIECE = SHARE + 8
FOLD = 4
F32 = jnp.float32


def place():
    row, col = lax.axis_index("row"), lax.axis_index("col")
    return row, col, col // 8, lax.rem(col, 8) // 2, lax.rem(col, 2)


def send(src, dst, out_sem, in_sem, to):
    copy = pltpu.make_async_remote_copy(
        src_ref=src, dst_ref=dst, send_sem=out_sem, recv_sem=in_sem,
        device_id=to, device_id_type=MESH,
    )
    copy.start()
    return copy


def arrival(slot, out_sem, in_sem, to):
    pltpu.make_async_remote_copy(
        src_ref=slot, dst_ref=slot, send_sem=out_sem, recv_sem=in_sem,
        device_id=to, device_id_type=MESH,
    ).wait_recv()


def beside(row, d):
    x, z = FAR_FIRST[d]
    return lax.rem(row // 4 + z, 2) * 4 + lax.rem(lax.rem(row, 4) + x, 4)


FAR_FIRST = ((0, 0), (2, 1), (1, 1), (3, 1), (2, 0), (0, 1), (1, 0), (3, 0))
RING = (2, 1, 3)


def greet(row, col, y, m):
    barrier = pltpu.get_barrier_semaphore()

    def signal(to):
        pl.semaphore_signal(barrier, inc=1, device_id=to, device_id_type=MESH)

    for d in (4, 3, 5, 2, 6, 1, 7):
        signal((row, y * 8 + lax.rem(m + d, 8)))
    for d in range(1, 8):
        signal((beside(row, d), col))
    for d in RING:
        signal((row, lax.rem(y + d, 4) * 8 + m))
    return barrier


PARTS = (pl.ds(0, 24), pl.ds(24, 16))


def gather_and_close(pivot, points, lists, closed, bt, ct, wt, own, listed, staged, rows, cols,
                     pivots, first_a, first_b, second_a, second_b, ka, wide, fold,
                     npd, npa, ncd, nra, wa, wb, wb2, own_sem,
                     s1, r1, s2, r2, s3, r3, s4, r4, sc, rc, sz, rz, sy, ry, sp, rp, sf, rf):
    row, col, y, zh, core = place()
    m = zh * 2 + core
    home = row * 4 + y
    mine = rows.at[y * 2 + core, zh]
    partner = (row, y * 8 + zh * 2 + 1 - core)
    first, second = (first_a, first_b), (second_a, second_b)

    load = [
        pltpu.make_async_copy(lists, listed, own_sem.at[0]),
        pltpu.make_async_copy(points, own.at[pl.ds(0, SHARE)], own_sem.at[1]),
    ]
    for copy in load:
        copy.start()
    barrier = greet(row, col, y, m)
    staged[...] = jnp.zeros_like(staged)
    load[0].wait()
    staged[:K, :SHARE] = listed[...].astype(F32)
    turned = pltpu.roll(staged[...], zh * SHARE, 1)
    own[SHARE:, :LANES] = turned[:8]
    own[SHARE:, LANES:] = turned[8:]
    load[1].wait()
    pl.semaphore_wait(barrier, 17)

    sent = []
    for h, part in enumerate(PARTS):
        for d in range(1, 8):
            to = (beside(row, d), col)
            sent.append(send(own.at[part], first[h].at[row], s1.at[h, d], r1.at[h, row], to))
    kept = [
        pltpu.make_async_copy(own.at[part], first[h].at[row], own_sem.at[2 + h])
        for h, part in enumerate(PARTS)
    ]
    kept.append(pltpu.make_async_copy(own, mine, own_sem.at[4]))
    for copy in kept:
        copy.start()
    for d in RING:
        to = (row, y * 8 + lax.rem(zh + d, 4) * 2 + core)
        sent.append(send(own, mine, sz.at[d], rz.at[zh], to))
    for copy in kept:
        copy.wait()
    for h in range(2):
        for d in range(1, 8):
            k = beside(row, d)
            arrival(first[h].at[k], s1.at[h, d], r1.at[h, k], (k, col))
        second[h][y] = first[h][pivot[0] // 4]
        for d in RING:
            to = (row, lax.rem(y + d, 4) * 8 + m)
            slot = second[h].at[y]
            sent.append(send(slot, slot, s2.at[h, d], r2.at[h, y], to))
    for h, part in enumerate(PARTS):
        for d in RING:
            k = lax.rem(y + d, 4)
            arrival(second[h].at[k], s2.at[h, d], r2.at[h, k], (row, k * 8 + m))
        pivots[core, zh, part] = second[h][lax.rem(pivot[0], 4)]
        piece = pivots.at[core, zh, part]
        for d in RING:
            to = (row, y * 8 + lax.rem(zh + d, 4) * 2 + core)
            sent.append(send(piece, piece, s3.at[h, d], r3.at[h, zh], to))

    stays = jnp.logical_and(home == col, row == m)
    given = cols.at[core, zh]
    taken = cols.at[lax.rem(row, 2), row // 2]
    out = pltpu.make_async_remote_copy(
        src_ref=own, dst_ref=given, send_sem=sc.at[0], recv_sem=rc.at[8],
        device_id=(m, home), device_id_type=MESH,
    )
    keep = pltpu.make_async_copy(own, given, own_sem.at[5])

    for d in RING:
        k = lax.rem(zh + d, 4)
        arrival(rows.at[y * 2 + core, k], sz.at[d], rz.at[k], (row, y * 8 + k * 2 + core))
    share = rows.at[y * 2 + core]
    for d in RING:
        to = (row, lax.rem(y + d, 4) * 8 + m)
        sent.append(send(share, share, sy.at[d], ry.at[y], to))

    for h, part in enumerate(PARTS):
        for d in RING:
            k = lax.rem(zh + d, 4)
            slot = pivots.at[core, k, part]
            arrival(slot, s3.at[h, d], r3.at[h, k], (row, y * 8 + k * 2 + core))
        half = pivots.at[core, :, part]
        sent.append(send(half, half, s4.at[h], r4.at[h], partner))
    sent.append(send(share, share, sp.at[0], rp.at[y], partner))
    for h, part in enumerate(PARTS):
        arrival(pivots.at[1 - core, :, part], s4.at[h], r4.at[h], partner)

    @pl.when(stays)
    def _():
        keep.start()

    @pl.when(jnp.logical_not(stays))
    def _():
        out.start()

    base, base_r, base_c = pivot[0] * PB, row * (4 * PB), col * PB
    norms_across(pivots, npa)
    norms_down(pivots, npd)
    note_lists(pivots, base, pivots, base, wa, wb)
    weigh(pivots, base, npd, pivots, base, npa, ka, wa, wb, 0, 1)
    spread(ka, wide)
    folded(wide, fold.at[0], 0, PB // FOLD)
    top = core * LANES

    def square(turn, meanwhile):
        old, new = turn % 2, (turn + 1) % 2

        def done(at, best):
            best = [reduced(b) for b in best]
            for g in range(2 * FOLD):
                wide[g, at, :] = best[g]
            for tile in range(2):
                part = gathered(best[FOLD * tile : FOLD * tile + FOLD])
                ka[tile, at, :] = jnp.minimum(ka[tile, at, :], part)

        min_plus(ka, fold.at[old], FOLD, done, 32, lambda t: top + 32 * t, 0, 4)
        half = LANES // FOLD
        low = pl.multiple_of(core * half, half)
        folded(wide.at[:, pl.ds(pl.multiple_of(top, LANES), LANES)], fold.at[new], low, half)
        ours = fold.at[new, :, pl.ds(low, half)]
        theirs = fold.at[new, :, pl.ds(pl.multiple_of(half - low, half), half)]
        copy = send(ours, ours, sf.at[new], rf.at[new], partner)
        meanwhile()
        arrival(theirs, sf.at[new], rf.at[new], partner)
        copy.wait_send()

    def forward():
        for d in (1, 3, 2):
            k = lax.rem(y + d, 4)
            share = rows.at[k * 2 + core]
            arrival(share, sy.at[d], ry.at[k], (row, k * 8 + m))
            sent.append(send(share, share, sp.at[d], rp.at[k], partner))

    def relay():
        @pl.when(stays)
        def _():
            keep.wait()

        @pl.when(jnp.logical_not(stays))
        def _():
            out.wait_send()
            arrival(taken, sc.at[0], rc.at[8], (col // 4, lax.rem(col, 4) * 8 + row))

        for d in range(1, 8):
            sent.append(send(taken, taken, sc.at[d], rc.at[row], (beside(row, d), col)))

    def panel():
        for d in range(1, 8):
            k = beside(row, d)
            arrival(cols.at[lax.rem(k, 2), k // 2], sc.at[d], rc.at[k], (k, col))
        norms_down(cols, ncd)
        note_lists(cols, base_c, pivots, base, wa, wb)
        weigh(cols, base_c, ncd, pivots, base, npa, bt, wa, wb, 0, 1)

    def row_weights():
        for k in range(4):
            arrival(rows.at[k * 2 + 1 - core], sp.at[k], rp.at[k], partner)
        norms_across(rows, nra)
        note_lists(pivots, base, rows, base_r, wa, wb2)
        weigh(pivots, base, npd, rows, base_r, nra, ct, wa, wb2, 0, 4)

    def tile_weights():
        note_lists(cols, base_c, rows, base_r, wa, wb2)
        weigh(cols, base_c, ncd, rows, base_r, nra, wt, wa, wb2, 0, 2)

    def more_tile_weights():
        weigh(cols, base_c, ncd, rows, base_r, nra, wt, wa, wb2, 2, 4)

    def first_work():
        forward()
        relay()

    def last_work():
        tile_weights()
        more_tile_weights()

    square(0, first_work)
    square(1, row_weights)
    square(2, panel)
    square(3, last_work)
    closed[...] = fold[(SQUARINGS + 1) % 2]
    for copy in sent:
        copy.wait_send()


def prepared(pivot, points, lists):
    sem = pltpu.SemaphoreType.DMA
    vmem = pl.BlockSpec(memory_space=pltpu.VMEM)
    hbm = pl.BlockSpec(memory_space=pltpu.HBM)
    i32 = jnp.int32
    return pl.pallas_call(
        gather_and_close,
        out_shape=[
            jax.ShapeDtypeStruct((2 * FOLD, PB // FOLD, LANES), F32),
            jax.ShapeDtypeStruct((2, PB, LANES), F32),
            jax.ShapeDtypeStruct((8, PB, LANES), F32),
            jax.ShapeDtypeStruct((8, PB, LANES), F32),
        ],
        in_specs=[pl.BlockSpec(memory_space=pltpu.SMEM), hbm, hbm],
        out_specs=[vmem] * 4,
        scratch_shapes=[
            pltpu.VMEM((PIECE, PB), F32),
            pltpu.VMEM((K, SHARE), i32),
            pltpu.VMEM((16, LANES), F32),
            pltpu.VMEM((8, 4, PIECE, PB), F32),
            pltpu.VMEM((2, 4, PIECE, PB), F32),
            pltpu.VMEM((2, 4, PIECE, PB), F32),
            pltpu.VMEM((8, PARTS[0].size, PB), F32),
            pltpu.VMEM((8, PARTS[1].size, PB), F32),
            pltpu.VMEM((4, PARTS[0].size, PB), F32),
            pltpu.VMEM((4, PARTS[1].size, PB), F32),
            pltpu.VMEM((2, PB, LANES), F32),
            pltpu.VMEM((2 * FOLD, PB, LANES), F32),
            pltpu.VMEM((2, 2 * FOLD, PB // FOLD, LANES), F32),
            pltpu.VMEM((PB, LANES), F32),
            pltpu.VMEM((2, 8, LANES), F32),
            pltpu.VMEM((PB, LANES), F32),
            pltpu.VMEM((8, 8, LANES), F32),
            pltpu.VMEM((PB, LANES), i32),
            pltpu.VMEM((2, 8, LANES), i32),
            pltpu.VMEM((8, 8, LANES), i32),
            sem((6,)),
            sem((2, 8)), sem((2, 8)), sem((2, 4)), sem((2, 4)), sem((2, 4)), sem((2, 4)),
            sem((2,)), sem((2,)),
            sem((8,)), sem((9,)), sem((4,)), sem((4,)), sem((4,)), sem((4,)),
            sem((4,)), sem((4,)), sem((2,)), sem((2,)),
        ],
        compiler_params=pltpu.CompilerParams(
            collective_id=0, has_side_effects=True, vmem_limit_bytes=32 << 20
        ),
    )(pivot, points, lists)


def dot(a, b, dims):
    return lax.dot_general(
        a, b, (dims, ((), ())),
        precision=lax.Precision.HIGHEST, preferred_element_type=F32,
    )


def points_of(pieces, tile):
    return pieces[tile, :, :SHARE, :].reshape(LANES, PB)


def lists_of(pieces, tile):
    both = pieces[tile, 0, SHARE:, :]
    for zh in range(1, 4):
        both = both + pieces[tile, zh, SHARE:, :]
    both = both.astype(jnp.int32)
    return jnp.concatenate([both[:, :LANES], both[:, LANES:]], axis=0)


def norms_down(points, out):
    for tile in range(2):
        p = points_of(points, tile)
        out[tile * LANES : (tile + 1) * LANES, :] = dot(
            p * p, jnp.ones((PB, LANES), F32), ((1,), (0,))
        )


def norms_across(points, out):
    def chunk(t, carry):
        p = points_of(points, t)
        out[t] = dot(jnp.ones((8, PB), F32), p * p, ((1,), (1,)))
        return carry

    lax.fori_loop(0, points.shape[0], chunk, 0)


def bits_of(lists, base, words):
    word = lax.broadcasted_iota(jnp.int32, (words, LANES), 0)
    found = jnp.zeros((words, LANES), jnp.int32)
    for slot in range(K):
        at = lists[slot : slot + 1, :] - base
        bit = jnp.left_shift(jnp.int32(1), at & 31)
        found = found | jnp.where(jnp.right_shift(at, 5) == word, bit, 0)
    return found


def lanes_of(piece, index):
    dims = lax.GatherDimensionNumbers(
        offset_dims=(), collapsed_slice_dims=(1,), start_index_map=(1,),
        operand_batching_dims=(0,), start_indices_batching_dims=(0,),
    )
    return lax.gather(
        piece, index[:, :, None], dims, (1, 1), mode=lax.GatherScatterMode.PROMISE_IN_BOUNDS
    )


def note_lists(down_of, base_a, across_of, base_b, wa, wb):
    tiles = across_of.shape[0]
    for tile in range(2):
        bits = bits_of(lists_of(down_of, tile), base_b, 4 * tiles)
        pad = jnp.zeros((LANES - 4 * tiles, LANES), jnp.int32)
        wa[tile * LANES : (tile + 1) * LANES, :] = jnp.concatenate([bits, pad], axis=0).T

    def words(t, carry):
        wb[t] = bits_of(lists_of(across_of, t), base_a, 8)
        return carry

    lax.fori_loop(0, tiles, words, 0)


def weigh(down_of, base_a, norm_a, across_of, base_b, norm_b, out, wa, wb, first, last):
    lane = lax.broadcasted_iota(jnp.int32, (32, LANES), 1)
    inside = lane & 31
    across = (lane // 32) * 64 + inside
    down = lax.broadcasted_iota(jnp.int32, (32, LANES), 0)

    def pair(n, carry):
        a = jnp.concatenate([points_of(down_of, 0), points_of(down_of, 1)], axis=0)
        b = jnp.concatenate([points_of(across_of, 2 * n), points_of(across_of, 2 * n + 1)], axis=0)
        inner = dot(a, b, ((1,), (1,)))
        for g in range(8):
            rows = slice(g * 32, g * 32 + 32)
            word_b = (g % 4) * 2 + g // 4
            for core in range(2):
                t, word_a = 2 * n + core, n * 8 + core
                part = inner[rows, core * LANES : (core + 1) * LANES]
                squares = norm_a[rows, :] + jnp.tile(norm_b[t], (4, 1)) - 2.0 * part
                squares = jnp.maximum(squares, 0.0)
                length = squares * lax.rsqrt(jnp.maximum(squares, 1.2e-38))
                listed = lanes_of(wa[rows, :], (lane // 32) * 2 + word_a)
                listed = jnp.right_shift(listed, inside)
                lists = jnp.tile(wb[t, pl.ds(word_b, 8, stride=0), :], (4, 1))
                listed = listed | jnp.right_shift(lists, down)
                weighted = jnp.where((listed & 1) == 1, length, far_weight * length)
                same = (down - across) == (base_b - base_a + 32 * (word_a - word_b))
                out[t, rows, :] = jnp.where(same, 0.0, weighted)
        return carry

    lax.fori_loop(first, last, pair, 0)


def min_plus(left, right, fold, done, rows, start_of, first, last):
    tiles = right.shape[0]
    halves = left.shape[0]
    depth = right.shape[1] // halves
    subs = rows // 8
    pattern = lax.broadcasted_iota(jnp.int32, (8, LANES), 1) // (LANES // fold)

    def block(t, carry):
        def rows_of(s):
            return pl.ds(pl.multiple_of(start_of(t) + 8 * s, 8), 8)

        def half(h, best):
            best = list(best)
            pieces = [left[h, rows_of(s), :] for s in range(subs)]
            for q in range(depth):
                downs = [lanes_of(piece, pattern + q * fold) for piece in pieces]
                for tile in range(tiles):
                    row = right[tile, pl.ds(h * depth + q, 8, stride=0), :]
                    for s in range(subs):
                        n = tile * subs + s
                        best[n] = jnp.minimum(best[n], downs[s] + row)
            return tuple(best)

        best = tuple(jnp.full((8, LANES), jnp.inf, F32) for _ in range(tiles * subs))
        best = lax.fori_loop(0, halves, half, best)
        for s in range(subs):
            done(rows_of(s), [best[tile * subs + s] for tile in range(tiles)])
        return carry

    lax.fori_loop(first, last, block, 0)


def folded(wide, right, low, count):
    lane = lax.broadcasted_iota(jnp.int32, (count, LANES), 1) // (LANES // FOLD)
    for tile in range(wide.shape[0]):
        piece = wide[tile, pl.ds(0, count, stride=FOLD), :]
        for c in range(1, FOLD):
            other = wide[tile, pl.ds(c, count, stride=FOLD), :]
            piece = jnp.where(lane == c, other, piece)
        right[tile, pl.ds(low, count), :] = piece


def gathered(parts):
    group = lax.broadcasted_iota(jnp.int32, parts[0].shape, 1) // (LANES // FOLD)
    tile = parts[0]
    for c in range(1, FOLD):
        tile = jnp.where(group == c, parts[c], tile)
    return tile


def reduced(piece):
    piece = jnp.minimum(piece, pltpu.roll(piece, 64, 1))
    return jnp.minimum(piece, pltpu.roll(piece, 32, 1))


def spread(tiles, wide):
    lane = lax.broadcasted_iota(jnp.int32, (32, LANES), 1) & 31

    def chunk(t, carry):
        rows = pl.ds(pl.multiple_of(t * 32, 32), 32)
        for g in range(wide.shape[0]):
            wide[g, rows, :] = lanes_of(tiles[g // FOLD, rows, :], lane + 32 * (g % FOLD))
        return carry

    lax.fori_loop(0, PB // 32, chunk, 0)


def body(fold, bt, ct, wt, o_ref, xt, ot):
    def done(at, best):
        best = [reduced(b) for b in best]
        for tile in range(2):
            kept = gathered(best[FOLD * tile : FOLD * tile + FOLD])
            xt[tile, at, :] = jnp.minimum(bt[tile, at, :], kept)

    min_plus(bt, fold, FOLD, done, 32, lambda t: 32 * t, 0, 8)

    def done(at, best):
        for tile in range(8):
            ot[tile, at, :] = jnp.minimum(wt[tile, at, :], best[tile])

    min_plus(xt, ct, 1, done, 32, lambda t: 32 * t, 0, 8)
    for t in range(8):
        for n in range(2):
            parts = [
                ot[t, (m % 2) * LANES + (m // 2) * 32 : (m % 2) * LANES + (m // 2) * 32 + 32, :]
                for m in range(4 * n, 4 * n + 4)
            ]
            flat = jnp.concatenate(parts, axis=0).T
            for zh in range(4):
                top = (t // 2) * 256 + (2 * zh + t % 2) * 32
                o_ref[top : top + 32, n * LANES : (n + 1) * LANES] = flat[zh * 32 : zh * 32 + 32]


def tile_of(closed, bt, ct, wt):
    vmem = pl.BlockSpec(memory_space=pltpu.VMEM)
    tiles = ct.shape[0]
    return pl.pallas_call(
        body,
        out_shape=jax.ShapeDtypeStruct((tiles * LANES, PB), F32),
        in_specs=[vmem] * 4,
        out_specs=vmem,
        scratch_shapes=[
            pltpu.VMEM((2, PB, LANES), F32),
            pltpu.VMEM((tiles, PB, LANES), F32),
        ],
        compiler_params=pltpu.CompilerParams(vmem_limit_bytes=24 << 20),
    )(closed, bt, ct, wt)


def local(features, neighbors, pivot):
    features = pltpu.with_memory_space_constraint(features, pltpu.HBM)
    lists = pltpu.with_memory_space_constraint(neighbors.T, pltpu.HBM)
    return tile_of(*prepared(pivot, features, lists))


def solution(mesh):
    return jax.shard_map(
        local,
        mesh=mesh,
        in_specs=(P(("row", "col"), None), P(("row", "col"), None), P()),
        out_specs=P("row", "col"),
        check_vma=False,
    )
```

```python
import functools

import jax
import jax.numpy as jnp
from jax import lax
from jax.experimental import pallas as pl
from jax.experimental.pallas import tpu as pltpu
from jax.sharding import PartitionSpec as P

MESH = pl.DeviceIdType.MESH
PB = 256
SQUARINGS = 3
K = 10
far_weight = 3.0
LANES = 128
SHARE = 32
PIECE = SHARE + 8
FOLD = 4
F32 = jnp.float32


def place():
    row, col = lax.axis_index("row"), lax.axis_index("col")
    return row, col, col // 8, lax.rem(col, 8) // 2, lax.rem(col, 2)


def send(src, dst, out_sem, in_sem, to):
    copy = pltpu.make_async_remote_copy(
        src_ref=src, dst_ref=dst, send_sem=out_sem, recv_sem=in_sem,
        device_id=to, device_id_type=MESH,
    )
    copy.start()
    return copy


def arrival(slot, out_sem, in_sem, to):
    pltpu.make_async_remote_copy(
        src_ref=slot, dst_ref=slot, send_sem=out_sem, recv_sem=in_sem,
        device_id=to, device_id_type=MESH,
    ).wait_recv()


def beside(row, d):
    x, z = FAR_FIRST[d]
    return lax.rem(row // 4 + z, 2) * 4 + lax.rem(lax.rem(row, 4) + x, 4)


FAR_FIRST = ((0, 0), (2, 1), (1, 1), (3, 1), (2, 0), (0, 1), (1, 0), (3, 0))
RING = (2, 1, 3)


def greet(row, col, y, m):
    barrier = pltpu.get_barrier_semaphore()

    def signal(to):
        pl.semaphore_signal(barrier, inc=1, device_id=to, device_id_type=MESH)

    for d in (4, 3, 5, 2, 6, 1, 7):
        signal((row, y * 8 + lax.rem(m + d, 8)))
    for d in range(1, 8):
        signal((beside(row, d), col))
    for d in RING:
        signal((row, lax.rem(y + d, 4) * 8 + m))
    return barrier


PARTS = (pl.ds(0, 24), pl.ds(24, 16))


def gather_and_close(pivot, points, lists, closed, bt, ct, wt, own, listed, staged, rows, cols,
                     pivots, first_a, first_b, second_a, second_b, ka, wide, fold,
                     npd, npa, ncd, nra, wa, wb, wb2, own_sem,
                     s1, r1, s2, r2, s3, r3, s4, r4, sc, rc, sz, rz, sy, ry, sp, rp, sf, rf):
    row, col, y, zh, core = place()
    m = zh * 2 + core
    home = row * 4 + y
    mine = rows.at[y * 2 + core, zh]
    partner = (row, y * 8 + zh * 2 + 1 - core)
    first, second = (first_a, first_b), (second_a, second_b)

    load = [
        pltpu.make_async_copy(lists, listed, own_sem.at[0]),
        pltpu.make_async_copy(points, own.at[pl.ds(0, SHARE)], own_sem.at[1]),
    ]
    for copy in load:
        copy.start()
    barrier = greet(row, col, y, m)
    staged[...] = jnp.zeros_like(staged)
    load[0].wait()
    staged[:K, :SHARE] = listed[...].astype(F32)
    turned = pltpu.roll(staged[...], zh * SHARE, 1)
    own[SHARE:, :LANES] = turned[:8]
    own[SHARE:, LANES:] = turned[8:]
    load[1].wait()
    pl.semaphore_wait(barrier, 17)

    sent = []
    for h, part in enumerate(PARTS):
        for d in range(1, 8):
            to = (beside(row, d), col)
            sent.append(send(own.at[part], first[h].at[row], s1.at[h, d], r1.at[h, row], to))
    kept = [
        pltpu.make_async_copy(own.at[part], first[h].at[row], own_sem.at[2 + h])
        for h, part in enumerate(PARTS)
    ]
    kept.append(pltpu.make_async_copy(own, mine, own_sem.at[4]))
    for copy in kept:
        copy.start()
    for copy in kept:
        copy.wait()
    for h in range(2):
        for d in range(1, 8):
            k = beside(row, d)
            arrival(first[h].at[k], s1.at[h, d], r1.at[h, k], (k, col))
        second[h][y] = first[h][pivot[0] // 4]
        for d in RING:
            to = (row, lax.rem(y + d, 4) * 8 + m)
            slot = second[h].at[y]
            sent.append(send(slot, slot, s2.at[h, d], r2.at[h, y], to))
    for d in RING:
        to = (row, y * 8 + lax.rem(zh + d, 4) * 2 + core)
        sent.append(send(own, mine, sz.at[d], rz.at[zh], to))
    for h, part in enumerate(PARTS):
        for d in RING:
            k = lax.rem(y + d, 4)
            arrival(second[h].at[k], s2.at[h, d], r2.at[h, k], (row, k * 8 + m))
        pivots[core, zh, part] = second[h][lax.rem(pivot[0], 4)]
        piece = pivots.at[core, zh, part]
        for d in RING:
            to = (row, y * 8 + lax.rem(zh + d, 4) * 2 + core)
            sent.append(send(piece, piece, s3.at[h, d], r3.at[h, zh], to))

    stays = jnp.logical_and(home == col, row == m)
    given = cols.at[core, zh]
    taken = cols.at[lax.rem(row, 2), row // 2]
    out = pltpu.make_async_remote_copy(
        src_ref=own, dst_ref=given, send_sem=sc.at[0], recv_sem=rc.at[8],
        device_id=(m, home), device_id_type=MESH,
    )
    keep = pltpu.make_async_copy(own, given, own_sem.at[5])

    for d in RING:
        k = lax.rem(zh + d, 4)
        arrival(rows.at[y * 2 + core, k], sz.at[d], rz.at[k], (row, y * 8 + k * 2 + core))
    share = rows.at[y * 2 + core]
    for d in RING:
        to = (row, lax.rem(y + d, 4) * 8 + m)
        sent.append(send(share, share, sy.at[d], ry.at[y], to))

    for h, part in enumerate(PARTS):
        for d in RING:
            k = lax.rem(zh + d, 4)
            slot = pivots.at[core, k, part]
            arrival(slot, s3.at[h, d], r3.at[h, k], (row, y * 8 + k * 2 + core))
        half = pivots.at[core, :, part]
        sent.append(send(half, half, s4.at[h], r4.at[h], partner))
    sent.append(send(share, share, sp.at[0], rp.at[y], partner))
    for h, part in enumerate(PARTS):
        arrival(pivots.at[1 - core, :, part], s4.at[h], r4.at[h], partner)

    @pl.when(stays)
    def _():
        keep.start()

    @pl.when(jnp.logical_not(stays))
    def _():
        out.start()

    base, base_r, base_c = pivot[0] * PB, row * (4 * PB), col * PB
    norms_across(pivots, npa)
    norms_down(pivots, npd)
    note_lists(pivots, base, pivots, base, wa, wb)
    weigh(pivots, base, npd, pivots, base, npa, ka, wa, wb, 0, 1)
    spread(ka, wide)
    folded(wide, fold.at[0], 0, PB // FOLD)
    top = core * LANES

    def square(turn, meanwhile):
        old, new = turn % 2, (turn + 1) % 2

        def done(at, best):
            best = [reduced(b) for b in best]
            for g in range(2 * FOLD):
                wide[g, at, :] = best[g]
            for tile in range(2):
                part = gathered(best[FOLD * tile : FOLD * tile + FOLD])
                ka[tile, at, :] = jnp.minimum(ka[tile, at, :], part)

        min_plus(ka, fold.at[old], FOLD, done, 32, lambda t: top + 32 * t, 0, 4)
        half = LANES // FOLD
        low = pl.multiple_of(core * half, half)
        folded(wide.at[:, pl.ds(pl.multiple_of(top, LANES), LANES)], fold.at[new], low, half)
        ours = fold.at[new, :, pl.ds(low, half)]
        theirs = fold.at[new, :, pl.ds(pl.multiple_of(half - low, half), half)]
        copy = send(ours, ours, sf.at[new], rf.at[new], partner)
        meanwhile()
        arrival(theirs, sf.at[new], rf.at[new], partner)
        copy.wait_send()

    def forward():
        for d in (1, 3, 2):
            k = lax.rem(y + d, 4)
            share = rows.at[k * 2 + core]
            arrival(share, sy.at[d], ry.at[k], (row, k * 8 + m))
            sent.append(send(share, share, sp.at[d], rp.at[k], partner))

    def relay():
        @pl.when(stays)
        def _():
            keep.wait()

        @pl.when(jnp.logical_not(stays))
        def _():
            out.wait_send()
            arrival(taken, sc.at[0], rc.at[8], (col // 4, lax.rem(col, 4) * 8 + row))

        for d in range(1, 8):
            sent.append(send(taken, taken, sc.at[d], rc.at[row], (beside(row, d), col)))

    def panel():
        for d in range(1, 8):
            k = beside(row, d)
            arrival(cols.at[lax.rem(k, 2), k // 2], sc.at[d], rc.at[k], (k, col))
        norms_down(cols, ncd)
        note_lists(cols, base_c, pivots, base, wa, wb)
        weigh(cols, base_c, ncd, pivots, base, npa, bt, wa, wb, 0, 1)

    def row_weights():
        for k in range(4):
            arrival(rows.at[k * 2 + 1 - core], sp.at[k], rp.at[k], partner)
        norms_across(rows, nra)
        note_lists(pivots, base, rows, base_r, wa, wb2)
        weigh(pivots, base, npd, rows, base_r, nra, ct, wa, wb2, 0, 4)

    def tile_weights():
        note_lists(cols, base_c, rows, base_r, wa, wb2)
        weigh(cols, base_c, ncd, rows, base_r, nra, wt, wa, wb2, 0, 2)

    def more_tile_weights():
        weigh(cols, base_c, ncd, rows, base_r, nra, wt, wa, wb2, 2, 4)

    def first_work():
        forward()
        relay()

    def last_work():
        tile_weights()
        more_tile_weights()

    square(0, first_work)
    square(1, row_weights)
    square(2, panel)
    square(3, last_work)
    closed[...] = fold[(SQUARINGS + 1) % 2]
    for copy in sent:
        copy.wait_send()


def prepared(pivot, points, lists):
    sem = pltpu.SemaphoreType.DMA
    vmem = pl.BlockSpec(memory_space=pltpu.VMEM)
    hbm = pl.BlockSpec(memory_space=pltpu.HBM)
    i32 = jnp.int32
    return pl.pallas_call(
        gather_and_close,
        out_shape=[
            jax.ShapeDtypeStruct((2 * FOLD, PB // FOLD, LANES), F32),
            jax.ShapeDtypeStruct((2, PB, LANES), F32),
            jax.ShapeDtypeStruct((8, PB, LANES), F32),
            jax.ShapeDtypeStruct((8, PB, LANES), F32),
        ],
        in_specs=[pl.BlockSpec(memory_space=pltpu.SMEM), hbm, hbm],
        out_specs=[vmem] * 4,
        scratch_shapes=[
            pltpu.VMEM((PIECE, PB), F32),
            pltpu.VMEM((K, SHARE), i32),
            pltpu.VMEM((16, LANES), F32),
            pltpu.VMEM((8, 4, PIECE, PB), F32),
            pltpu.VMEM((2, 4, PIECE, PB), F32),
            pltpu.VMEM((2, 4, PIECE, PB), F32),
            pltpu.VMEM((8, PARTS[0].size, PB), F32),
            pltpu.VMEM((8, PARTS[1].size, PB), F32),
            pltpu.VMEM((4, PARTS[0].size, PB), F32),
            pltpu.VMEM((4, PARTS[1].size, PB), F32),
            pltpu.VMEM((2, PB, LANES), F32),
            pltpu.VMEM((2 * FOLD, PB, LANES), F32),
            pltpu.VMEM((2, 2 * FOLD, PB // FOLD, LANES), F32),
            pltpu.VMEM((PB, LANES), F32),
            pltpu.VMEM((2, 8, LANES), F32),
            pltpu.VMEM((PB, LANES), F32),
            pltpu.VMEM((8, 8, LANES), F32),
            pltpu.VMEM((PB, LANES), i32),
            pltpu.VMEM((2, 8, LANES), i32),
            pltpu.VMEM((8, 8, LANES), i32),
            sem((6,)),
            sem((2, 8)), sem((2, 8)), sem((2, 4)), sem((2, 4)), sem((2, 4)), sem((2, 4)),
            sem((2,)), sem((2,)),
            sem((8,)), sem((9,)), sem((4,)), sem((4,)), sem((4,)), sem((4,)),
            sem((4,)), sem((4,)), sem((2,)), sem((2,)),
        ],
        compiler_params=pltpu.CompilerParams(
            collective_id=0, has_side_effects=True, vmem_limit_bytes=32 << 20
        ),
    )(pivot, points, lists)


def dot(a, b, dims):
    return lax.dot_general(
        a, b, (dims, ((), ())),
        precision=lax.Precision.HIGHEST, preferred_element_type=F32,
    )


def points_of(pieces, tile):
    return pieces[tile, :, :SHARE, :].reshape(LANES, PB)


def lists_of(pieces, tile):
    both = pieces[tile, 0, SHARE:, :]
    for zh in range(1, 4):
        both = both + pieces[tile, zh, SHARE:, :]
    both = both.astype(jnp.int32)
    return jnp.concatenate([both[:, :LANES], both[:, LANES:]], axis=0)


def norms_down(points, out):
    for tile in range(2):
        p = points_of(points, tile)
        out[tile * LANES : (tile + 1) * LANES, :] = dot(
            p * p, jnp.ones((PB, LANES), F32), ((1,), (0,))
        )


def norms_across(points, out):
    def chunk(t, carry):
        p = points_of(points, t)
        out[t] = dot(jnp.ones((8, PB), F32), p * p, ((1,), (1,)))
        return carry

    lax.fori_loop(0, points.shape[0], chunk, 0)


def bits_of(lists, base, words):
    word = lax.broadcasted_iota(jnp.int32, (words, LANES), 0)
    found = jnp.zeros((words, LANES), jnp.int32)
    for slot in range(K):
        at = lists[slot : slot + 1, :] - base
        bit = jnp.left_shift(jnp.int32(1), at & 31)
        found = found | jnp.where(jnp.right_shift(at, 5) == word, bit, 0)
    return found


def lanes_of(piece, index):
    dims = lax.GatherDimensionNumbers(
        offset_dims=(), collapsed_slice_dims=(1,), start_index_map=(1,),
        operand_batching_dims=(0,), start_indices_batching_dims=(0,),
    )
    return lax.gather(
        piece, index[:, :, None], dims, (1, 1), mode=lax.GatherScatterMode.PROMISE_IN_BOUNDS
    )


def note_lists(down_of, base_a, across_of, base_b, wa, wb):
    tiles = across_of.shape[0]
    for tile in range(2):
        bits = bits_of(lists_of(down_of, tile), base_b, 4 * tiles)
        pad = jnp.zeros((LANES - 4 * tiles, LANES), jnp.int32)
        wa[tile * LANES : (tile + 1) * LANES, :] = jnp.concatenate([bits, pad], axis=0).T

    def words(t, carry):
        wb[t] = bits_of(lists_of(across_of, t), base_a, 8)
        return carry

    lax.fori_loop(0, tiles, words, 0)


def weigh(down_of, base_a, norm_a, across_of, base_b, norm_b, out, wa, wb, first, last):
    lane = lax.broadcasted_iota(jnp.int32, (32, LANES), 1)
    inside = lane & 31
    across = (lane // 32) * 64 + inside
    down = lax.broadcasted_iota(jnp.int32, (32, LANES), 0)

    def pair(n, carry):
        a = jnp.concatenate([points_of(down_of, 0), points_of(down_of, 1)], axis=0)
        b = jnp.concatenate([points_of(across_of, 2 * n), points_of(across_of, 2 * n + 1)], axis=0)
        inner = dot(a, b, ((1,), (1,)))
        for g in range(8):
            rows = slice(g * 32, g * 32 + 32)
            word_b = (g % 4) * 2 + g // 4
            for core in range(2):
                t, word_a = 2 * n + core, n * 8 + core
                part = inner[rows, core * LANES : (core + 1) * LANES]
                squares = norm_a[rows, :] + jnp.tile(norm_b[t], (4, 1)) - 2.0 * part
                squares = jnp.maximum(squares, 0.0)
                length = squares * lax.rsqrt(jnp.maximum(squares, 1.2e-38))
                listed = lanes_of(wa[rows, :], (lane // 32) * 2 + word_a)
                listed = jnp.right_shift(listed, inside)
                lists = jnp.tile(wb[t, pl.ds(word_b, 8, stride=0), :], (4, 1))
                listed = listed | jnp.right_shift(lists, down)
                weighted = jnp.where((listed & 1) == 1, length, far_weight * length)
                same = (down - across) == (base_b - base_a + 32 * (word_a - word_b))
                out[t, rows, :] = jnp.where(same, 0.0, weighted)
        return carry

    lax.fori_loop(first, last, pair, 0)


def min_plus(left, right, fold, done, rows, start_of, first, last):
    tiles = right.shape[0]
    halves = left.shape[0]
    depth = right.shape[1] // halves
    subs = rows // 8
    pattern = lax.broadcasted_iota(jnp.int32, (8, LANES), 1) // (LANES // fold)

    def block(t, carry):
        def rows_of(s):
            return pl.ds(pl.multiple_of(start_of(t) + 8 * s, 8), 8)

        def half(h, best):
            best = list(best)
            pieces = [left[h, rows_of(s), :] for s in range(subs)]
            for q in range(depth):
                downs = [lanes_of(piece, pattern + q * fold) for piece in pieces]
                for tile in range(tiles):
                    row = right[tile, pl.ds(h * depth + q, 8, stride=0), :]
                    for s in range(subs):
                        n = tile * subs + s
                        best[n] = jnp.minimum(best[n], downs[s] + row)
            return tuple(best)

        best = tuple(jnp.full((8, LANES), jnp.inf, F32) for _ in range(tiles * subs))
        best = lax.fori_loop(0, halves, half, best)
        for s in range(subs):
            done(rows_of(s), [best[tile * subs + s] for tile in range(tiles)])
        return carry

    lax.fori_loop(first, last, block, 0)


def folded(wide, right, low, count):
    lane = lax.broadcasted_iota(jnp.int32, (count, LANES), 1) // (LANES // FOLD)
    for tile in range(wide.shape[0]):
        piece = wide[tile, pl.ds(0, count, stride=FOLD), :]
        for c in range(1, FOLD):
            other = wide[tile, pl.ds(c, count, stride=FOLD), :]
            piece = jnp.where(lane == c, other, piece)
        right[tile, pl.ds(low, count), :] = piece


def gathered(parts):
    group = lax.broadcasted_iota(jnp.int32, parts[0].shape, 1) // (LANES // FOLD)
    tile = parts[0]
    for c in range(1, FOLD):
        tile = jnp.where(group == c, parts[c], tile)
    return tile


def reduced(piece):
    piece = jnp.minimum(piece, pltpu.roll(piece, 64, 1))
    return jnp.minimum(piece, pltpu.roll(piece, 32, 1))


def spread(tiles, wide):
    lane = lax.broadcasted_iota(jnp.int32, (32, LANES), 1) & 31

    def chunk(t, carry):
        rows = pl.ds(pl.multiple_of(t * 32, 32), 32)
        for g in range(wide.shape[0]):
            wide[g, rows, :] = lanes_of(tiles[g // FOLD, rows, :], lane + 32 * (g % FOLD))
        return carry

    lax.fori_loop(0, PB // 32, chunk, 0)


def body(fold, bt, ct, wt, o_ref, xt, ot):
    def done(at, best):
        best = [reduced(b) for b in best]
        for tile in range(2):
            kept = gathered(best[FOLD * tile : FOLD * tile + FOLD])
            xt[tile, at, :] = jnp.minimum(bt[tile, at, :], kept)

    min_plus(bt, fold, FOLD, done, 32, lambda t: 32 * t, 0, 8)

    def done(at, best):
        for tile in range(8):
            ot[tile, at, :] = jnp.minimum(wt[tile, at, :], best[tile])

    min_plus(xt, ct, 1, done, 32, lambda t: 32 * t, 0, 8)
    for t in range(8):
        for n in range(2):
            parts = [
                ot[t, (m % 2) * LANES + (m // 2) * 32 : (m % 2) * LANES + (m // 2) * 32 + 32, :]
                for m in range(4 * n, 4 * n + 4)
            ]
            flat = jnp.concatenate(parts, axis=0).T
            for zh in range(4):
                top = (t // 2) * 256 + (2 * zh + t % 2) * 32
                o_ref[top : top + 32, n * LANES : (n + 1) * LANES] = flat[zh * 32 : zh * 32 + 32]


def tile_of(closed, bt, ct, wt):
    vmem = pl.BlockSpec(memory_space=pltpu.VMEM)
    tiles = ct.shape[0]
    return pl.pallas_call(
        body,
        out_shape=jax.ShapeDtypeStruct((tiles * LANES, PB), F32),
        in_specs=[vmem] * 4,
        out_specs=vmem,
        scratch_shapes=[
            pltpu.VMEM((2, PB, LANES), F32),
            pltpu.VMEM((tiles, PB, LANES), F32),
        ],
        compiler_params=pltpu.CompilerParams(vmem_limit_bytes=24 << 20),
    )(closed, bt, ct, wt)


def local(features, neighbors, pivot):
    features = pltpu.with_memory_space_constraint(features, pltpu.HBM)
    lists = pltpu.with_memory_space_constraint(neighbors.T, pltpu.HBM)
    return tile_of(*prepared(pivot, features, lists))


def solution(mesh):
    return jax.shard_map(
        local,
        mesh=mesh,
        in_specs=(P(("row", "col"), None), P(("row", "col"), None), P()),
        out_specs=P("row", "col"),
        check_vma=False,
    )
```

```python
import functools

import jax
import jax.numpy as jnp
from jax import lax
from jax.experimental import pallas as pl
from jax.experimental.pallas import tpu as pltpu
from jax.sharding import PartitionSpec as P

MESH = pl.DeviceIdType.MESH
PB = 256
SQUARINGS = 3
K = 10
far_weight = 3.0
LANES = 128
SHARE = 32
PIECE = SHARE + 8
FOLD = 4
F32 = jnp.float32


def place():
    row, col = lax.axis_index("row"), lax.axis_index("col")
    return row, col, col // 8, lax.rem(col, 8) // 2, lax.rem(col, 2)


def send(src, dst, out_sem, in_sem, to):
    copy = pltpu.make_async_remote_copy(
        src_ref=src, dst_ref=dst, send_sem=out_sem, recv_sem=in_sem,
        device_id=to, device_id_type=MESH,
    )
    copy.start()
    return copy


def arrival(slot, out_sem, in_sem, to):
    pltpu.make_async_remote_copy(
        src_ref=slot, dst_ref=slot, send_sem=out_sem, recv_sem=in_sem,
        device_id=to, device_id_type=MESH,
    ).wait_recv()


def beside(row, d):
    x, z = FAR_FIRST[d]
    return lax.rem(row // 4 + z, 2) * 4 + lax.rem(lax.rem(row, 4) + x, 4)


FAR_FIRST = ((0, 0), (2, 1), (1, 1), (3, 1), (2, 0), (0, 1), (1, 0), (3, 0))
RING = (2, 1, 3)


def greet(row, col, y, m):
    barrier = pltpu.get_barrier_semaphore()

    def signal(to):
        pl.semaphore_signal(barrier, inc=1, device_id=to, device_id_type=MESH)

    for d in (4, 3, 5, 2, 6, 1, 7):
        signal((row, y * 8 + lax.rem(m + d, 8)))
    for d in range(1, 8):
        signal((beside(row, d), col))
    for d in RING:
        signal((row, lax.rem(y + d, 4) * 8 + m))
    return barrier


PARTS = (pl.ds(0, 16), pl.ds(16, 24))


def gather_and_close(pivot, points, lists, closed, bt, ct, wt, own, listed, staged, rows, cols,
                     pivots, first_a, first_b, second_a, second_b, ka, wide, fold,
                     npd, npa, ncd, nra, wa, wb, wb2, own_sem,
                     s1, r1, s2, r2, s3, r3, s4, r4, sc, rc, sz, rz, sy, ry, sp, rp, sf, rf):
    row, col, y, zh, core = place()
    m = zh * 2 + core
    home = row * 4 + y
    mine = rows.at[y * 2 + core, zh]
    partner = (row, y * 8 + zh * 2 + 1 - core)
    first, second = (first_a, first_b), (second_a, second_b)

    load = [
        pltpu.make_async_copy(lists, listed, own_sem.at[0]),
        pltpu.make_async_copy(points, own.at[pl.ds(0, SHARE)], own_sem.at[1]),
    ]
    for copy in load:
        copy.start()
    barrier = greet(row, col, y, m)
    staged[...] = jnp.zeros_like(staged)
    load[0].wait()
    staged[:K, :SHARE] = listed[...].astype(F32)
    turned = pltpu.roll(staged[...], zh * SHARE, 1)
    own[SHARE:, :LANES] = turned[:8]
    own[SHARE:, LANES:] = turned[8:]
    load[1].wait()
    pl.semaphore_wait(barrier, 17)

    sent = []
    for h, part in enumerate(PARTS):
        for d in range(1, 8):
            to = (beside(row, d), col)
            sent.append(send(own.at[part], first[h].at[row], s1.at[h, d], r1.at[h, row], to))
    kept = [
        pltpu.make_async_copy(own.at[part], first[h].at[row], own_sem.at[2 + h])
        for h, part in enumerate(PARTS)
    ]
    kept.append(pltpu.make_async_copy(own, mine, own_sem.at[4]))
    for copy in kept:
        copy.start()
    for copy in kept:
        copy.wait()
    for h in range(2):
        for d in range(1, 8):
            k = beside(row, d)
            arrival(first[h].at[k], s1.at[h, d], r1.at[h, k], (k, col))
        second[h][y] = first[h][pivot[0] // 4]
        for d in RING:
            to = (row, lax.rem(y + d, 4) * 8 + m)
            slot = second[h].at[y]
            sent.append(send(slot, slot, s2.at[h, d], r2.at[h, y], to))
    for d in RING:
        to = (row, y * 8 + lax.rem(zh + d, 4) * 2 + core)
        sent.append(send(own, mine, sz.at[d], rz.at[zh], to))
    for h, part in enumerate(PARTS):
        for d in RING:
            k = lax.rem(y + d, 4)
            arrival(second[h].at[k], s2.at[h, d], r2.at[h, k], (row, k * 8 + m))
        pivots[core, zh, part] = second[h][lax.rem(pivot[0], 4)]
        piece = pivots.at[core, zh, part]
        for d in RING:
            to = (row, y * 8 + lax.rem(zh + d, 4) * 2 + core)
            sent.append(send(piece, piece, s3.at[h, d], r3.at[h, zh], to))

    stays = jnp.logical_and(home == col, row == m)
    given = cols.at[core, zh]
    taken = cols.at[lax.rem(row, 2), row // 2]
    out = pltpu.make_async_remote_copy(
        src_ref=own, dst_ref=given, send_sem=sc.at[0], recv_sem=rc.at[8],
        device_id=(m, home), device_id_type=MESH,
    )
    keep = pltpu.make_async_copy(own, given, own_sem.at[5])

    for d in RING:
        k = lax.rem(zh + d, 4)
        arrival(rows.at[y * 2 + core, k], sz.at[d], rz.at[k], (row, y * 8 + k * 2 + core))
    share = rows.at[y * 2 + core]
    for d in RING:
        to = (row, lax.rem(y + d, 4) * 8 + m)
        sent.append(send(share, share, sy.at[d], ry.at[y], to))

    for h, part in enumerate(PARTS):
        for d in RING:
            k = lax.rem(zh + d, 4)
            slot = pivots.at[core, k, part]
            arrival(slot, s3.at[h, d], r3.at[h, k], (row, y * 8 + k * 2 + core))
        half = pivots.at[core, :, part]
        sent.append(send(half, half, s4.at[h], r4.at[h], partner))
    sent.append(send(share, share, sp.at[0], rp.at[y], partner))
    for h, part in enumerate(PARTS):
        arrival(pivots.at[1 - core, :, part], s4.at[h], r4.at[h], partner)

    @pl.when(stays)
    def _():
        keep.start()

    @pl.when(jnp.logical_not(stays))
    def _():
        out.start()

    base, base_r, base_c = pivot[0] * PB, row * (4 * PB), col * PB
    norms_across(pivots, npa)
    norms_down(pivots, npd)
    note_lists(pivots, base, pivots, base, wa, wb)
    weigh(pivots, base, npd, pivots, base, npa, ka, wa, wb, 0, 1)
    spread(ka, wide)
    folded(wide, fold.at[0], 0, PB // FOLD)
    top = core * LANES

    def square(turn, meanwhile):
        old, new = turn % 2, (turn + 1) % 2

        def done(at, best):
            best = [reduced(b) for b in best]
            for g in range(2 * FOLD):
                wide[g, at, :] = best[g]
            for tile in range(2):
                part = gathered(best[FOLD * tile : FOLD * tile + FOLD])
                ka[tile, at, :] = jnp.minimum(ka[tile, at, :], part)

        min_plus(ka, fold.at[old], FOLD, done, 32, lambda t: top + 32 * t, 0, 4)
        half = LANES // FOLD
        low = pl.multiple_of(core * half, half)
        folded(wide.at[:, pl.ds(pl.multiple_of(top, LANES), LANES)], fold.at[new], low, half)
        ours = fold.at[new, :, pl.ds(low, half)]
        theirs = fold.at[new, :, pl.ds(pl.multiple_of(half - low, half), half)]
        copy = send(ours, ours, sf.at[new], rf.at[new], partner)
        meanwhile()
        arrival(theirs, sf.at[new], rf.at[new], partner)
        copy.wait_send()

    def forward():
        for d in (1, 3, 2):
            k = lax.rem(y + d, 4)
            share = rows.at[k * 2 + core]
            arrival(share, sy.at[d], ry.at[k], (row, k * 8 + m))
            sent.append(send(share, share, sp.at[d], rp.at[k], partner))

    def relay():
        @pl.when(stays)
        def _():
            keep.wait()

        @pl.when(jnp.logical_not(stays))
        def _():
            out.wait_send()
            arrival(taken, sc.at[0], rc.at[8], (col // 4, lax.rem(col, 4) * 8 + row))

        for d in range(1, 8):
            sent.append(send(taken, taken, sc.at[d], rc.at[row], (beside(row, d), col)))

    def panel():
        for d in range(1, 8):
            k = beside(row, d)
            arrival(cols.at[lax.rem(k, 2), k // 2], sc.at[d], rc.at[k], (k, col))
        norms_down(cols, ncd)
        note_lists(cols, base_c, pivots, base, wa, wb)
        weigh(cols, base_c, ncd, pivots, base, npa, bt, wa, wb, 0, 1)

    def row_weights():
        for k in range(4):
            arrival(rows.at[k * 2 + 1 - core], sp.at[k], rp.at[k], partner)
        norms_across(rows, nra)
        note_lists(pivots, base, rows, base_r, wa, wb2)
        weigh(pivots, base, npd, rows, base_r, nra, ct, wa, wb2, 0, 4)

    def tile_weights():
        note_lists(cols, base_c, rows, base_r, wa, wb2)
        weigh(cols, base_c, ncd, rows, base_r, nra, wt, wa, wb2, 0, 2)

    def more_tile_weights():
        weigh(cols, base_c, ncd, rows, base_r, nra, wt, wa, wb2, 2, 4)

    def first_work():
        forward()
        relay()

    def last_work():
        tile_weights()
        more_tile_weights()

    square(0, first_work)
    square(1, row_weights)
    square(2, panel)
    square(3, last_work)
    closed[...] = fold[(SQUARINGS + 1) % 2]
    for copy in sent:
        copy.wait_send()


def prepared(pivot, points, lists):
    sem = pltpu.SemaphoreType.DMA
    vmem = pl.BlockSpec(memory_space=pltpu.VMEM)
    hbm = pl.BlockSpec(memory_space=pltpu.HBM)
    i32 = jnp.int32
    return pl.pallas_call(
        gather_and_close,
        out_shape=[
            jax.ShapeDtypeStruct((2 * FOLD, PB // FOLD, LANES), F32),
            jax.ShapeDtypeStruct((2, PB, LANES), F32),
            jax.ShapeDtypeStruct((8, PB, LANES), F32),
            jax.ShapeDtypeStruct((8, PB, LANES), F32),
        ],
        in_specs=[pl.BlockSpec(memory_space=pltpu.SMEM), hbm, hbm],
        out_specs=[vmem] * 4,
        scratch_shapes=[
            pltpu.VMEM((PIECE, PB), F32),
            pltpu.VMEM((K, SHARE), i32),
            pltpu.VMEM((16, LANES), F32),
            pltpu.VMEM((8, 4, PIECE, PB), F32),
            pltpu.VMEM((2, 4, PIECE, PB), F32),
            pltpu.VMEM((2, 4, PIECE, PB), F32),
            pltpu.VMEM((8, PARTS[0].size, PB), F32),
            pltpu.VMEM((8, PARTS[1].size, PB), F32),
            pltpu.VMEM((4, PARTS[0].size, PB), F32),
            pltpu.VMEM((4, PARTS[1].size, PB), F32),
            pltpu.VMEM((2, PB, LANES), F32),
            pltpu.VMEM((2 * FOLD, PB, LANES), F32),
            pltpu.VMEM((2, 2 * FOLD, PB // FOLD, LANES), F32),
            pltpu.VMEM((PB, LANES), F32),
            pltpu.VMEM((2, 8, LANES), F32),
            pltpu.VMEM((PB, LANES), F32),
            pltpu.VMEM((8, 8, LANES), F32),
            pltpu.VMEM((PB, LANES), i32),
            pltpu.VMEM((2, 8, LANES), i32),
            pltpu.VMEM((8, 8, LANES), i32),
            sem((6,)),
            sem((2, 8)), sem((2, 8)), sem((2, 4)), sem((2, 4)), sem((2, 4)), sem((2, 4)),
            sem((2,)), sem((2,)),
            sem((8,)), sem((9,)), sem((4,)), sem((4,)), sem((4,)), sem((4,)),
            sem((4,)), sem((4,)), sem((2,)), sem((2,)),
        ],
        compiler_params=pltpu.CompilerParams(
            collective_id=0, has_side_effects=True, vmem_limit_bytes=32 << 20
        ),
    )(pivot, points, lists)


def dot(a, b, dims):
    return lax.dot_general(
        a, b, (dims, ((), ())),
        precision=lax.Precision.HIGHEST, preferred_element_type=F32,
    )


def points_of(pieces, tile):
    return pieces[tile, :, :SHARE, :].reshape(LANES, PB)


def lists_of(pieces, tile):
    both = pieces[tile, 0, SHARE:, :]
    for zh in range(1, 4):
        both = both + pieces[tile, zh, SHARE:, :]
    both = both.astype(jnp.int32)
    return jnp.concatenate([both[:, :LANES], both[:, LANES:]], axis=0)


def norms_down(points, out):
    for tile in range(2):
        p = points_of(points, tile)
        out[tile * LANES : (tile + 1) * LANES, :] = dot(
            p * p, jnp.ones((PB, LANES), F32), ((1,), (0,))
        )


def norms_across(points, out):
    def chunk(t, carry):
        p = points_of(points, t)
        out[t] = dot(jnp.ones((8, PB), F32), p * p, ((1,), (1,)))
        return carry

    lax.fori_loop(0, points.shape[0], chunk, 0)


def bits_of(lists, base, words):
    word = lax.broadcasted_iota(jnp.int32, (words, LANES), 0)
    found = jnp.zeros((words, LANES), jnp.int32)
    for slot in range(K):
        at = lists[slot : slot + 1, :] - base
        bit = jnp.left_shift(jnp.int32(1), at & 31)
        found = found | jnp.where(jnp.right_shift(at, 5) == word, bit, 0)
    return found


def lanes_of(piece, index):
    dims = lax.GatherDimensionNumbers(
        offset_dims=(), collapsed_slice_dims=(1,), start_index_map=(1,),
        operand_batching_dims=(0,), start_indices_batching_dims=(0,),
    )
    return lax.gather(
        piece, index[:, :, None], dims, (1, 1), mode=lax.GatherScatterMode.PROMISE_IN_BOUNDS
    )


def note_lists(down_of, base_a, across_of, base_b, wa, wb):
    tiles = across_of.shape[0]
    for tile in range(2):
        bits = bits_of(lists_of(down_of, tile), base_b, 4 * tiles)
        pad = jnp.zeros((LANES - 4 * tiles, LANES), jnp.int32)
        wa[tile * LANES : (tile + 1) * LANES, :] = jnp.concatenate([bits, pad], axis=0).T

    def words(t, carry):
        wb[t] = bits_of(lists_of(across_of, t), base_a, 8)
        return carry

    lax.fori_loop(0, tiles, words, 0)


def weigh(down_of, base_a, norm_a, across_of, base_b, norm_b, out, wa, wb, first, last):
    lane = lax.broadcasted_iota(jnp.int32, (32, LANES), 1)
    inside = lane & 31
    across = (lane // 32) * 64 + inside
    down = lax.broadcasted_iota(jnp.int32, (32, LANES), 0)

    def pair(n, carry):
        a = jnp.concatenate([points_of(down_of, 0), points_of(down_of, 1)], axis=0)
        b = jnp.concatenate([points_of(across_of, 2 * n), points_of(across_of, 2 * n + 1)], axis=0)
        inner = dot(a, b, ((1,), (1,)))
        for g in range(8):
            rows = slice(g * 32, g * 32 + 32)
            word_b = (g % 4) * 2 + g // 4
            for core in range(2):
                t, word_a = 2 * n + core, n * 8 + core
                part = inner[rows, core * LANES : (core + 1) * LANES]
                squares = norm_a[rows, :] + jnp.tile(norm_b[t], (4, 1)) - 2.0 * part
                squares = jnp.maximum(squares, 0.0)
                length = squares * lax.rsqrt(jnp.maximum(squares, 1.2e-38))
                listed = lanes_of(wa[rows, :], (lane // 32) * 2 + word_a)
                listed = jnp.right_shift(listed, inside)
                lists = jnp.tile(wb[t, pl.ds(word_b, 8, stride=0), :], (4, 1))
                listed = listed | jnp.right_shift(lists, down)
                weighted = jnp.where((listed & 1) == 1, length, far_weight * length)
                same = (down - across) == (base_b - base_a + 32 * (word_a - word_b))
                out[t, rows, :] = jnp.where(same, 0.0, weighted)
        return carry

    lax.fori_loop(first, last, pair, 0)


def min_plus(left, right, fold, done, rows, start_of, first, last):
    tiles = right.shape[0]
    halves = left.shape[0]
    depth = right.shape[1] // halves
    subs = rows // 8
    pattern = lax.broadcasted_iota(jnp.int32, (8, LANES), 1) // (LANES // fold)

    def block(t, carry):
        def rows_of(s):
            return pl.ds(pl.multiple_of(start_of(t) + 8 * s, 8), 8)

        def half(h, best):
            best = list(best)
            pieces = [left[h, rows_of(s), :] for s in range(subs)]
            for q in range(depth):
                downs = [lanes_of(piece, pattern + q * fold) for piece in pieces]
                for tile in range(tiles):
                    row = right[tile, pl.ds(h * depth + q, 8, stride=0), :]
                    for s in range(subs):
                        n = tile * subs + s
                        best[n] = jnp.minimum(best[n], downs[s] + row)
            return tuple(best)

        best = tuple(jnp.full((8, LANES), jnp.inf, F32) for _ in range(tiles * subs))
        best = lax.fori_loop(0, halves, half, best)
        for s in range(subs):
            done(rows_of(s), [best[tile * subs + s] for tile in range(tiles)])
        return carry

    lax.fori_loop(first, last, block, 0)


def folded(wide, right, low, count):
    lane = lax.broadcasted_iota(jnp.int32, (count, LANES), 1) // (LANES // FOLD)
    for tile in range(wide.shape[0]):
        piece = wide[tile, pl.ds(0, count, stride=FOLD), :]
        for c in range(1, FOLD):
            other = wide[tile, pl.ds(c, count, stride=FOLD), :]
            piece = jnp.where(lane == c, other, piece)
        right[tile, pl.ds(low, count), :] = piece


def gathered(parts):
    group = lax.broadcasted_iota(jnp.int32, parts[0].shape, 1) // (LANES // FOLD)
    tile = parts[0]
    for c in range(1, FOLD):
        tile = jnp.where(group == c, parts[c], tile)
    return tile


def reduced(piece):
    piece = jnp.minimum(piece, pltpu.roll(piece, 64, 1))
    return jnp.minimum(piece, pltpu.roll(piece, 32, 1))


def spread(tiles, wide):
    lane = lax.broadcasted_iota(jnp.int32, (32, LANES), 1) & 31

    def chunk(t, carry):
        rows = pl.ds(pl.multiple_of(t * 32, 32), 32)
        for g in range(wide.shape[0]):
            wide[g, rows, :] = lanes_of(tiles[g // FOLD, rows, :], lane + 32 * (g % FOLD))
        return carry

    lax.fori_loop(0, PB // 32, chunk, 0)


def body(fold, bt, ct, wt, o_ref, xt, ot):
    def done(at, best):
        best = [reduced(b) for b in best]
        for tile in range(2):
            kept = gathered(best[FOLD * tile : FOLD * tile + FOLD])
            xt[tile, at, :] = jnp.minimum(bt[tile, at, :], kept)

    min_plus(bt, fold, FOLD, done, 32, lambda t: 32 * t, 0, 8)

    def done(at, best):
        for tile in range(8):
            ot[tile, at, :] = jnp.minimum(wt[tile, at, :], best[tile])

    min_plus(xt, ct, 1, done, 32, lambda t: 32 * t, 0, 8)
    for t in range(8):
        for n in range(2):
            parts = [
                ot[t, (m % 2) * LANES + (m // 2) * 32 : (m % 2) * LANES + (m // 2) * 32 + 32, :]
                for m in range(4 * n, 4 * n + 4)
            ]
            flat = jnp.concatenate(parts, axis=0).T
            for zh in range(4):
                top = (t // 2) * 256 + (2 * zh + t % 2) * 32
                o_ref[top : top + 32, n * LANES : (n + 1) * LANES] = flat[zh * 32 : zh * 32 + 32]


def tile_of(closed, bt, ct, wt):
    vmem = pl.BlockSpec(memory_space=pltpu.VMEM)
    tiles = ct.shape[0]
    return pl.pallas_call(
        body,
        out_shape=jax.ShapeDtypeStruct((tiles * LANES, PB), F32),
        in_specs=[vmem] * 4,
        out_specs=vmem,
        scratch_shapes=[
            pltpu.VMEM((2, PB, LANES), F32),
            pltpu.VMEM((tiles, PB, LANES), F32),
        ],
        compiler_params=pltpu.CompilerParams(vmem_limit_bytes=24 << 20),
    )(closed, bt, ct, wt)


def local(features, neighbors, pivot):
    features = pltpu.with_memory_space_constraint(features, pltpu.HBM)
    lists = pltpu.with_memory_space_constraint(neighbors.T, pltpu.HBM)
    return tile_of(*prepared(pivot, features, lists))


def solution(mesh):
    return jax.shard_map(
        local,
        mesh=mesh,
        in_specs=(P(("row", "col"), None), P(("row", "col"), None), P()),
        out_specs=P("row", "col"),
        check_vma=False,
    )
```
